768 devices in a mesh: gx: 24 (over z_hi, x, core), gy: 32 (over y, z_lo).
Axes of the slice: x: 4, y: 8, z: 12 (z_hi: 3, z_lo: 4; z = z_hi * 4 + z_lo), core: 2. Of those that a mesh axis runs over, the one named last changes fastest.
Arguments:
- populations: bfloat16 [2, 19, 384, 32768], P(None, None, 'gx', 'gy'), may hold values from 0 to 1, as said below
- wall_class: int32 [384, 32768], P('gx', 'gy'), may hold values from 0 to 3
- planes: int32 [2], replicated, may hold values from 0 to 383, as said below
Outputs:
- final_populations: bfloat16 [2, 19, 384, 32768], P(None, None, 'gx', 'gy')
The draws below stay inside these ranges and needn't reach their ends.
Inputs may be any that keep to these rules, and one draw needn't show every extreme that they name: `populations`: every entry is positive. planes[0] lies below 96; planes[1] is the last x plane, 383.
All inputs are finite; a program needn't handle non-finite values.
Results may differ from the reference program's by a relative error of at most 0.0029.
Values may be sent and summed in bfloat16 or wider, within the bound.
A program may use at most 32 MiB of HBM per device.

```python
import math
import jax
import jax.numpy as jnp

NZ = 64
STEPS = 2
NX = 384
NY = 512


velocities = ((0, 0, 0), (1, 0, 0), (-1, 0, 0), (0, 1, 0), (0, -1, 0), (0, 0, 1), (0, 0, -1), (1, 1, 0), (-1, -1, 0), (1, -1, 0), (-1, 1, 0), (1, 0, 1), (-1, 0, -1), (1, 0, -1), (-1, 0, 1), (0, 1, 1), (0, -1, -1), (0, 1, -1), (0, -1, 1))


lattice_weights = (1.0 / 3.0,) + (1.0 / 18.0,) * 6 + (1.0 / 36.0,) * 12


def draw_populations(key, part):
    key_phase, key_level, key_flow, key_noise = jax.random.split(jax.random.fold_in(key, 11), 4)
    blocks_x = (NX + 7) // 8
    blocks_y = (NY + 7) // 8
    phase_flag = jax.random.randint(key_phase, (blocks_x, blocks_y), 0, 2, dtype=jnp.int32) == 1
    unit_draw = jax.random.uniform(key_level, (2, 2, blocks_x, blocks_y), jnp.float32)
    rich_level = jnp.exp(math.log(1.2) + (math.log(1.5) - math.log(1.2)) * unit_draw[0])
    lean_level = jnp.exp(math.log(0.08) + (math.log(0.15) - math.log(0.08)) * unit_draw[1])
    oil_density = jnp.where(phase_flag, rich_level[0], lean_level[0])
    brine_density = jnp.where(phase_flag, lean_level[1], rich_level[1])
    block_density = jnp.stack([oil_density, brine_density])
    index_x = jnp.arange(NX, dtype=jnp.int32) // 8
    index_y = jnp.arange(NY * NZ, dtype=jnp.int32) // NZ // 8
    spread_x = jnp.take(block_density, index_x, axis=1)
    densities = jnp.take(spread_x, index_y, axis=2).reshape(2, 1, NX, NY * NZ)
    flows = jax.random.uniform(key_flow, (3, NX, NY * NZ), jnp.float32, -0.06, 0.06)
    noise = jax.random.uniform(key_noise, (2, 19, NX, NY * NZ), jnp.float32, 0.8, 1.2)
    table_x = jnp.array([vector[0] for vector in velocities], jnp.float32).reshape(19, 1, 1)
    table_y = jnp.array([vector[1] for vector in velocities], jnp.float32).reshape(19, 1, 1)
    table_z = jnp.array([vector[2] for vector in velocities], jnp.float32).reshape(19, 1, 1)
    weights = jnp.array(lattice_weights, jnp.float32).reshape(19, 1, 1)
    along = table_x * flows[0] + table_y * flows[1] + table_z * flows[2]
    values = weights * densities * (1.0 + 3.0 * along) * noise
    return values.astype(jnp.bfloat16)


def draw_wall_class(key, part):
    key_offset, key_thick, key_class, key_holes = jax.random.split(jax.random.fold_in(key, 23), 4)
    columns = jnp.arange(NY * NZ, dtype=jnp.int32).reshape(1, NY * NZ)
    rows_y = columns // NZ
    rows_z = columns % NZ
    offsets = jax.random.randint(key_offset, (NX, 1), 0, 12, dtype=jnp.int32)
    thickness = jax.random.randint(key_thick, (NX, 1), 2, 6, dtype=jnp.int32)
    phase = (rows_y + offsets + rows_z // 16) % 12
    solid = phase < thickness
    holes = jax.random.randint(key_holes, (NX, NY * NZ), 0, 16, dtype=jnp.int32) == 0
    classes = jax.random.randint(key_class, (NX, NY * NZ), 1, 4, dtype=jnp.int32)
    return jnp.where(jnp.logical_and(solid, jnp.logical_not(holes)), classes, 0).astype(jnp.int32)


def draw_planes(key, part):
    key_inlet = jax.random.fold_in(key, 37)
    inlet = jax.random.randint(key_inlet, (1,), 0, NX // 4, dtype=jnp.int32)
    outlet = jnp.full((1,), NX - 1, jnp.int32)
    return jnp.concatenate([inlet, outlet]).astype(jnp.int32)


def setup_inputs(seed: int = 0) -> dict:
    key_list = jax.random.split(jax.random.key(seed), 4)
    populations = draw_populations(jax.random.fold_in(key_list[3], 71), 0)
    wall_class = draw_wall_class(jax.random.fold_in(key_list[3], 71), 0)
    planes = draw_planes(jax.random.fold_in(key_list[3], 71), 0)
    return dict(populations=populations, wall_class=wall_class, planes=planes)


velocities = ((0, 0, 0), (1, 0, 0), (-1, 0, 0), (0, 1, 0), (0, -1, 0), (0, 0, 1), (0, 0, -1),
              (1, 1, 0), (-1, -1, 0), (1, -1, 0), (-1, 1, 0), (1, 0, 1), (-1, 0, -1),
              (1, 0, -1), (-1, 0, 1), (0, 1, 1), (0, -1, -1), (0, 1, -1), (0, -1, 1))
lattice_weights = (1.0 / 3.0,) + (1.0 / 18.0,) * 6 + (1.0 / 36.0,) * 12
COUPLING = 2.5
RELAX_TIMES = (1.0, 0.8)
STRENGTHS = (0.0, 0.15, 0.35, 0.6)
INLET_DENSITY = (1.0, 0.03)
OUTLET_DENSITY = (0.03, 1.0)


def opposite(direction):
    if direction == 0:
        return 0
    return direction + 1 if direction % 2 == 1 else direction - 1


def wall_strength(wall_class):
    total = jnp.zeros(wall_class.shape, jnp.float32)
    for level in range(1, 4):
        total = total + jnp.where(wall_class == level, jnp.float32(STRENGTHS[level]), jnp.float32(0.0))
    return total


def densities_of(pops):
    totals = []
    for component in range(2):
        total = pops[component, 0].astype(jnp.float32)
        for direction in range(1, 19):
            total = total + pops[component, direction].astype(jnp.float32)
        totals.append(total)
    return jnp.stack(totals)


def potential_of(densities, fluids):
    return jnp.where(fluids, 1.0 - jnp.exp(-densities), jnp.float32(0.0)).astype(jnp.float32)


def directional_sum(field, lookup):
    totals = [None, None, None]
    for direction in range(1, 19):
        moved = lookup(field, velocities[direction])
        for axis_pos in range(3):
            along = velocities[direction][axis_pos]
            if along != 0:
                term = (lattice_weights[direction] * along) * moved
                totals[axis_pos] = term if totals[axis_pos] is None else totals[axis_pos] + term
    return totals


def interaction(potential_centre, pulls, wall_pulls):
    forces = []
    for component in range(2):
        partner = 1 - component
        wetting = 1.0 if component == 0 else -1.0
        forces.append([-potential_centre[component] * (COUPLING * pulls[axis_pos][partner] + wetting * wall_pulls[axis_pos]) for axis_pos in range(3)])
    return forces


def collide(pops, densities, forces, fluids):
    momenta = []
    for component in range(2):
        parts = []
        for axis_pos in range(3):
            total = jnp.zeros(densities.shape[1:], jnp.float32)
            for direction in range(1, 19):
                along = velocities[direction][axis_pos]
                if along != 0:
                    total = total + along * pops[component, direction].astype(jnp.float32)
            parts.append(total)
        momenta.append(parts)
    weight_sum = densities[0] / RELAX_TIMES[0] + densities[1] / RELAX_TIMES[1]
    common = [(momenta[0][axis_pos] / RELAX_TIMES[0] + momenta[1][axis_pos] / RELAX_TIMES[1]) / weight_sum for axis_pos in range(3)]
    outputs = []
    for component in range(2):
        relax_time = RELAX_TIMES[component]
        velocity = [common[axis_pos] + relax_time * forces[component][axis_pos] / densities[component] for axis_pos in range(3)]
        square = velocity[0] * velocity[0] + velocity[1] * velocity[1] + velocity[2] * velocity[2]
        for direction in range(19):
            vector = velocities[direction]
            along = vector[0] * velocity[0] + vector[1] * velocity[1] + vector[2] * velocity[2]
            equilibrium = lattice_weights[direction] * densities[component] * (1.0 + 3.0 * along + 4.5 * along * along - 1.5 * square)
            current = pops[component, direction].astype(jnp.float32)
            relaxed = current - (current - equilibrium) / relax_time
            bounced = pops[component, opposite(direction)]
            outputs.append(jnp.where(fluids, relaxed.astype(jnp.bfloat16), bounced))
    return jnp.stack(outputs).reshape((2, 19) + densities.shape[1:])


def stream(collided, lookup):
    outputs = []
    for component in range(2):
        for direction in range(19):
            vector = velocities[direction]
            outputs.append(lookup(collided[component, direction], (-vector[0], -vector[1], -vector[2])))
    return jnp.stack(outputs).reshape((2, 19) + outputs[0].shape)


def reset(pops, xglobal, fluids, planes):
    at_inlet = jnp.logical_and(xglobal == planes[0], fluids)
    at_outlet = jnp.logical_and(xglobal == planes[1], fluids)
    outputs = []
    for component in range(2):
        for direction in range(19):
            inlet_value = jnp.asarray(lattice_weights[direction] * INLET_DENSITY[component], jnp.bfloat16)
            outlet_value = jnp.asarray(lattice_weights[direction] * OUTLET_DENSITY[component], jnp.bfloat16)
            outputs.append(jnp.where(at_inlet, inlet_value, jnp.where(at_outlet, outlet_value, pops[component, direction])))
    return jnp.stack(outputs).reshape(pops.shape)


def periodic(field, vector):
    return jnp.roll(field, (-vector[0], -vector[1], -vector[2]), axis=(-3, -2, -1))


def reference(populations, wall_class, planes):
    current = populations.reshape(2, 19, NX, NY, NZ)
    classes = wall_class.reshape(NX, NY, NZ)
    fluids = classes == 0
    wall_field = wall_strength(classes)
    xglobal = jnp.arange(NX, dtype=jnp.int32).reshape(NX, 1, 1)
    wall_pulls = directional_sum(wall_field, periodic)
    for repeat in range(STEPS):
        densities = densities_of(current)
        potential = potential_of(densities, fluids)
        pulls = directional_sum(potential, periodic)
        forces = interaction(potential, pulls, wall_pulls)
        collided = collide(current, densities, forces, fluids)
        read = stream(collided, periodic)
        current = reset(read, xglobal, fluids, planes)
    return current.reshape(2, 19, NX, NY * NZ)
```

```python
import functools

import jax
import jax.numpy as jnp
import numpy as np
from jax import lax
from jax.experimental import pallas as pl
from jax.experimental.pallas import tpu as pltpu
from jax.sharding import PartitionSpec as P

NZ = 64
STEPS = 2
MESH = pl.DeviceIdType.MESH
velocities = (
    (0, 0, 0),
    (1, 0, 0),
    (-1, 0, 0),
    (0, 1, 0),
    (0, -1, 0),
    (0, 0, 1),
    (0, 0, -1),
    (1, 1, 0),
    (-1, -1, 0),
    (1, -1, 0),
    (-1, 1, 0),
    (1, 0, 1),
    (-1, 0, -1),
    (1, 0, -1),
    (-1, 0, 1),
    (0, 1, 1),
    (0, -1, -1),
    (0, 1, -1),
    (0, -1, 1),
)
lattice_weights = (1.0 / 3.0,) + (1.0 / 18.0,) * 6 + (1.0 / 36.0,) * 12
COUPLING = 2.5
RELAX_TIMES = (1.0, 0.8)
STRENGTHS = (0.0, 0.15, 0.35, 0.6)
INLET_DENSITY = (1.0, 0.03)
OUTLET_DENSITY = (0.03, 1.0)
along_x = ((1, 7, 9, 11, 13), (2, 8, 10, 12, 14))
along_y = ((3, 7, 10, 15, 17), (4, 8, 9, 16, 18))
along_edge = {(0, 0): 7, (1, 1): 8, (0, 1): 9, (1, 0): 10}
EDGES = ((0, 0), (0, 1), (1, 0), (1, 1))

HALO = 8


def opposite(direction):
    if direction == 0:
        return 0
    return direction + 1 if direction % 2 == 1 else direction - 1


def kernel(
    nx_devices,
    ny_devices,
    pops_hbm,
    wall_ref,
    planes_ref,
    out_ref,
    pops,
    field,
    spread,
    aux,
    stream,
    pot_sx,
    pot_sy,
    pot_rx,
    pot_ry,
    pot_rc,
    pop_sx,
    pop_sy,
    pop_rx,
    pop_ry,
    pop_rc,
    in_sem,
    send_sem,
    recv_sem,
):
    size_x = pops.shape[2]
    tiles = pops.shape[3] // 128
    halves = size_x // 8
    rows = size_x + 2 * HALO
    block = (tiles + 2) * rows
    f32 = jnp.float32
    bf16 = jnp.bfloat16

    gx = lax.axis_index("gx")
    gy = lax.axis_index("gy")
    near_x = (lax.rem(gx + 1, nx_devices), lax.rem(gx + nx_devices - 1, nx_devices))
    near_y = (lax.rem(gy + 1, ny_devices), lax.rem(gy + ny_devices - 1, ny_devices))

    def load_in(t):
        lanes = pl.ds(pl.multiple_of(t * 128, 128), 128)
        return pltpu.make_async_copy(
            pops_hbm.at[:, :, :, lanes], pops.at[:, :, :, lanes], in_sem.at[t]
        )

    for t in range(tiles):
        load_in(t).start()

    barrier = pltpu.get_barrier_semaphore()
    targets = [(near_x[0], gy), (near_x[1], gy), (gx, near_y[0]), (gx, near_y[1])]
    targets += [(near_x[i], near_y[j]) for i, j in EDGES]
    for target in targets:
        pl.semaphore_signal(barrier, inc=1, device_id=target, device_id_type=MESH)

    lane = lax.broadcasted_iota(jnp.int32, (8, 128), 1)
    row_index = lax.broadcasted_iota(jnp.int32, (8, 128), 0)
    low = lane < NZ
    first_z = jnp.logical_or(lane == 0, lane == NZ)
    last_z = jnp.logical_or(lane == NZ - 1, lane == 2 * NZ - 1)

    def roll(value, by):
        return pltpu.roll(value, by % 128, 1)

    def z_from_below(value, turned):
        return roll(jnp.where(last_z, turned, value), 1)

    def z_from_above(value, turned):
        return roll(jnp.where(first_z, turned, value), -1)

    def at(index, tile, row):
        return pl.ds(pl.multiple_of(index * block + tile * rows + row, 8), 8)

    def off(index, tile, row):
        return pl.ds(index * block + tile * rows + row, 8)

    def across(index, row):
        return pl.ds(index * block + rows + row, tiles, stride=rows)

    def spot(t, half):
        return pl.ds(pl.multiple_of(t * size_x + half * 8, 8), 8)

    def fluid_at(t, half):
        lanes = pl.ds(pl.multiple_of(t * 128, 128), 128)
        return wall_ref[half * 8 : half * 8 + 8, lanes]

    def pop_at(component, direction, t, half):
        lanes = pl.ds(pl.multiple_of(t * 128, 128), 128)
        return pops[component, direction, half * 8 : half * 8 + 8, lanes].astype(f32)

    def store_potential(t, half, densities):
        wall = fluid_at(t, half)
        fluid = wall == 0
        strength = jnp.where(
            wall == 1, STRENGTHS[1], jnp.where(wall == 2, STRENGTHS[2], STRENGTHS[3])
        )
        oil = COUPLING * (1.0 - jnp.exp(-densities[0]))
        brine = COUPLING * (1.0 - jnp.exp(-densities[1]))
        field[at(0, t + 1, HALO + half * 8), :] = jnp.where(fluid, brine, strength)
        field[at(1, t + 1, HALO + half * 8), :] = jnp.where(fluid, oil, -strength)
        aux[0, spot(t, half), :] = densities[0]
        aux[1, spot(t, half), :] = densities[1]

    def first_density(t, carry):
        load_in(t).wait()
        for half in range(halves):
            densities = []
            for component in range(2):
                total = pop_at(component, 0, t, half)
                for direction in range(1, 19):
                    total = total + pop_at(component, direction, t, half)
                densities.append(total)
            store_potential(t, half, densities)
        return carry

    def exchange(number, sends_x, sends_y, edge_source, recvs_x, recvs_y, recvs_c):
        copies = []
        for side in range(2):
            copies.append((sends_x.at[side], recvs_x.at[side], (near_x[side], gy)))
            copies.append((sends_y.at[side], recvs_y.at[side], (gx, near_y[side])))
        for place, (i, j) in enumerate(EDGES):
            copies.append((edge_source(i, j), recvs_c.at[place], (near_x[i], near_y[j])))
        started = []
        for place, (source, target, device) in enumerate(copies):
            copy = pltpu.make_async_remote_copy(
                src_ref=source,
                dst_ref=target,
                send_sem=send_sem.at[number, place],
                recv_sem=recv_sem.at[number, place],
                device_id=device,
                device_id_type=MESH,
            )
            copy.start()
            started.append(copy)
        return started

    def send_potential(step):
        for side in range(2):
            row = HALO + size_x - 1 if side == 0 else HALO
            tile = tiles if side == 0 else 1
            for index in range(2):
                pot_sx[step, side, index] = field[across(index, row), :].astype(bf16)
            for half in range(halves):
                one = field[at(0, tile, HALO + half * 8), :]
                two = field[at(1, tile, HALO + half * 8), :]
                if side == 0:
                    packed = jnp.where(low, roll(one, NZ), two)
                else:
                    packed = jnp.where(low, one, roll(two, NZ))
                pot_sy[step, side, half] = packed.astype(bf16)
        return exchange(
            2 * step,
            pot_sx.at[step],
            pot_sy.at[step],
            lambda i, j: pot_sy.at[step, j, halves - 1 if i == 0 else 0],
            pot_rx.at[step],
            pot_ry.at[step],
            pot_rc.at[step],
        )

    def common_velocity(t, carry):
        for half in range(halves):
            momenta = []
            for component in range(2):
                gap = [None] * 19
                for direction in range(1, 19, 2):
                    gap[direction] = pop_at(component, direction, t, half) - pop_at(
                        component, direction + 1, t, half
                    )
                momenta.append(
                    (
                        (gap[1] + gap[7]) + (gap[9] + gap[11]) + gap[13],
                        (gap[3] + gap[7]) + (gap[15] - gap[9]) + gap[17],
                        (gap[5] + gap[11]) + (gap[15] - gap[13]) - gap[17],
                    )
                )
            place = spot(t, half)
            inverse = 1.0 / (
                aux[0, place, :] * (1.0 / RELAX_TIMES[0]) + aux[1, place, :] * (1.0 / RELAX_TIMES[1])
            )
            for axis_pos in range(3):
                aux[2 + axis_pos, place, :] = (
                    momenta[0][axis_pos] * (1.0 / RELAX_TIMES[0])
                    + momenta[1][axis_pos] * (1.0 / RELAX_TIMES[1])
                ) * inverse
        return carry

    def receive_potential(step, copies):
        for copy in copies:
            copy.wait()
        for side in range(2):
            row = HALO - 1 if side == 0 else HALO + size_x
            tile = 0 if side == 0 else tiles + 1
            for index in range(2):
                field[across(index, row), :] = pot_rx[step, side, index].astype(f32)

            def unpack(value, start):
                turned = roll(value, NZ)
                one, two = (turned, value) if side == 0 else (value, turned)
                field[at(0, tile, start), :] = one
                field[at(1, tile, start), :] = two

            for half in range(halves):
                unpack(pot_ry[step, side, half].astype(f32), HALO + half * 8)
            for place, (i, j) in enumerate(EDGES):
                if j == side:
                    start = 0 if i == 0 else HALO + size_x
                    unpack(pot_rc[step, place].astype(f32), start)

    def spread_x(tile, carry):
        for half in range(halves):
            start = HALO + half * 8
            place = pl.ds(pl.multiple_of(tile * size_x + half * 8, 8), 8)
            for index in range(2):
                centre = field[at(index, tile, start), :]
                above = field[off(index, tile, start + 1), :]
                below = field[off(index, tile, start - 1), :]
                gap = above - below
                total = 2.0 * centre + (above + below)
                spread[5 * index, place, :] = gap
                spread[5 * index + 1, place, :] = total
                spread[5 * index + 2, place, :] = roll(gap, NZ)
                spread[5 * index + 3, place, :] = roll(total, NZ)
                spread[5 * index + 4, place, :] = roll(centre, NZ)
        return carry

    def pull_of(index, t, half):
        def held(kind, tile):
            place = pl.ds(pl.multiple_of(tile * size_x + half * 8, 8), 8)
            return spread[5 * index + kind, place, :]

        def upper(here, above):
            return jnp.where(low, here, above)

        def lower(here, below):
            return jnp.where(low, below, here)

        gap = held(0, t + 1)
        turned_gap = held(2, t + 1)
        pull_x = 2.0 * gap + (
            upper(turned_gap, held(2, t + 2)) + lower(turned_gap, held(2, t))
        )
        pull_x = pull_x + (z_from_below(gap, turned_gap) + z_from_above(gap, turned_gap))
        turned_total = held(3, t + 1)
        pull_y = upper(turned_total, held(3, t + 2)) - lower(turned_total, held(3, t))
        turned = held(4, t + 1)
        centre = field[at(index, t + 1, HALO + half * 8), :]
        y_above = upper(turned, held(4, t + 2))
        y_below = lower(turned, held(4, t))
        next_tile = field[at(index, t + 2, HALO + half * 8), :]
        previous_tile = field[at(index, t, HALO + half * 8), :]
        turned_y_above = jnp.where(low, next_tile, centre)
        turned_y_below = jnp.where(low, centre, previous_tile)
        gap_y = y_above - y_below
        turned_gap_y = turned_y_above - turned_y_below
        pull_y = pull_y + (z_from_below(gap_y, turned_gap_y) + z_from_above(gap_y, turned_gap_y))
        plane = held(1, t + 1) + (y_above + y_below)
        turned_plane = turned_total + (turned_y_above + turned_y_below)
        pull_z = z_from_above(plane, turned_plane) - z_from_below(plane, turned_plane)
        return pull_x, pull_y, pull_z

    def store_moved(component, direction, t, half, value):
        _, along, upward = velocities[direction]
        if along != 0 or upward != 0:
            turned = roll(value, NZ)
            if along != 0:
                value, turned = turned, value
            if upward == 1:
                value = z_from_below(value, turned)
            elif upward == -1:
                value = z_from_above(value, turned)
        stream[at(19 * component + direction, t + 1, HALO + half * 8), :] = value

    def collide(t, carry):
        for half in range(halves):
            place = spot(t, half)
            fluid = fluid_at(t, half) == 0
            centre = [field[at(index, t + 1, HALO + half * 8), :] for index in range(2)]
            for component in range(2):
                pull = pull_of(component, t, half)
                density = aux[component, place, :]
                scale = (-3.0 * RELAX_TIMES[component] / (36.0 * COUPLING)) * centre[1 - component]
                scale = scale / density
                speed = [
                    3.0 * aux[2 + axis_pos, place, :] + scale * pull[axis_pos] for axis_pos in range(3)
                ]
                square = speed[0] * speed[0] + speed[1] * speed[1] + speed[2] * speed[2]
                level = 1.0 - square * (1.0 / 6.0)
                rate = 1.0 / RELAX_TIMES[component]
                kept = 1.0 - rate
                light = density * (rate / 36.0)
                heavy = density * (rate / 18.0)
                light_level = light * level
                heavy_level = heavy * level

                def settle(direction, equilibrium, own, bounced):
                    relaxed = equilibrium if kept == 0.0 else equilibrium + kept * own
                    store_moved(
                        component, direction, t, half, jnp.where(fluid, relaxed, bounced)
                    )

                rest = pop_at(component, 0, t, half)
                settle(0, 6.0 * heavy_level, rest, rest)
                for direction in range(1, 19, 2):
                    along = None
                    for axis_pos in range(3):
                        part = velocities[direction][axis_pos]
                        if part == 1:
                            along = speed[axis_pos] if along is None else along + speed[axis_pos]
                        elif part == -1:
                            along = along - speed[axis_pos]
                    weighted = (heavy if direction < 7 else light) * along
                    even = (heavy_level if direction < 7 else light_level) + 0.5 * (weighted * along)
                    one = pop_at(component, direction, t, half)
                    two = pop_at(component, direction + 1, t, half)
                    settle(direction, even + weighted, one, two)
                    settle(direction + 1, even - weighted, two, one)
        return carry

    def send_populations(step):
        for side in range(2):
            row = HALO + size_x - 1 if side == 0 else HALO
            tile = tiles if side == 0 else 1
            for component in range(2):
                for place, direction in enumerate(along_x[side]):
                    pop_sx[step, side, 5 * component + place] = stream[
                        across(19 * component + direction, row), :
                    ].astype(bf16)
            for place, direction in enumerate(along_y[side]):
                for half in range(halves):
                    one = stream[at(direction, tile, HALO + half * 8), :]
                    two = stream[at(19 + direction, tile, HALO + half * 8), :]
                    if side == 0:
                        packed = jnp.where(low, one, roll(two, NZ))
                    else:
                        packed = jnp.where(low, roll(one, NZ), two)
                    pop_sy[step, side, place, half] = packed.astype(bf16)
        return exchange(
            2 * step + 1,
            pop_sx.at[step],
            pop_sy.at[step],
            lambda i, j: pop_sy.at[
                step, j, along_y[j].index(along_edge[i, j]), halves - 1 if i == 0 else 0
            ],
            pop_rx.at[step],
            pop_ry.at[step],
            pop_rc.at[step],
        )

    def receive_populations(step, copies):
        for copy in copies:
            copy.wait()
        for side in range(2):
            row = HALO - 1 if side == 0 else HALO + size_x
            tile = 0 if side == 0 else tiles + 1
            for component in range(2):
                for place, direction in enumerate(along_x[side]):
                    stream[across(19 * component + direction, row), :] = pop_rx[
                        step, side, 5 * component + place
                    ].astype(f32)

            def unpack(direction, value, start):
                turned = roll(value, NZ)
                one, two = (value, turned) if side == 0 else (turned, value)
                stream[at(direction, tile, start), :] = one
                stream[at(19 + direction, tile, start), :] = two

            for place, direction in enumerate(along_y[side]):
                for half in range(halves):
                    unpack(
                        direction, pop_ry[step, side, place, half].astype(f32), HALO + half * 8
                    )
            for place, (i, j) in enumerate(EDGES):
                if j == side:
                    start = 0 if i == 0 else HALO + size_x
                    unpack(along_edge[i, j], pop_rc[step, place].astype(f32), start)

    def settle_step(last):
        target = out_ref if last else pops

        def read(t, carry):
            lanes = pl.ds(pl.multiple_of(t * 128, 128), 128)
            for half in range(halves):
                fluid = fluid_at(t, half) == 0
                xglobal = gx * size_x + half * 8 + row_index
                inlet = jnp.logical_and(xglobal == planes_ref[0], fluid)
                outlet = jnp.logical_and(xglobal == planes_ref[1], fluid)
                fixed = jnp.logical_or(inlet, outlet)
                densities = []
                for component in range(2):
                    forced = {}
                    for weight in sorted(set(lattice_weights)):
                        values = [
                            float(np.asarray(weight * level[component], jnp.bfloat16))
                            for level in (INLET_DENSITY, OUTLET_DENSITY)
                        ]
                        forced[weight] = jnp.where(inlet, values[0], values[1])
                    total = None
                    for direction in range(19):
                        step_x, step_y, _ = velocities[direction]
                        index = 19 * component + direction
                        start = HALO + half * 8 - step_x
                        value = stream[off(index, t + 1, start), :]
                        if step_y == 1:
                            value = jnp.where(low, stream[off(index, t, start), :], value)
                        elif step_y == -1:
                            value = jnp.where(low, value, stream[off(index, t + 2, start), :])
                        value = jnp.where(fixed, forced[lattice_weights[direction]], value)
                        narrow = value.astype(bf16)
                        target[component, direction, half * 8 : half * 8 + 8, lanes] = narrow
                        if not last:
                            wide = narrow.astype(f32)
                            total = wide if total is None else total + wide
                    densities.append(total)
                if not last:
                    store_potential(t, half, densities)
            return carry

        lax.fori_loop(0, tiles, read, 0)

    lax.fori_loop(0, tiles, first_density, 0)
    pl.semaphore_wait(barrier, len(targets))
    for step in range(STEPS):
        copies = send_potential(step)
        lax.fori_loop(0, tiles, common_velocity, 0)
        receive_potential(step, copies)
        lax.fori_loop(0, tiles + 2, spread_x, 0)
        lax.fori_loop(0, tiles, collide, 0)
        copies = send_populations(step)
        receive_populations(step, copies)
        settle_step(step == STEPS - 1)


def on_device(nx_devices, ny_devices, populations, wall_class, planes):
    size_x, width = populations.shape[2:]
    tiles = width // 128
    halves = size_x // 8
    rows = size_x + 2 * HALO
    block = (tiles + 2) * rows
    bf16 = jnp.bfloat16
    f32 = jnp.float32
    return pl.pallas_call(
        functools.partial(kernel, nx_devices, ny_devices),
        out_shape=jax.ShapeDtypeStruct(populations.shape, bf16),
        in_specs=[
            pl.BlockSpec(memory_space=pl.ANY),
            pl.BlockSpec(memory_space=pltpu.VMEM),
            pl.BlockSpec(memory_space=pltpu.SMEM),
        ],
        out_specs=pl.BlockSpec(memory_space=pltpu.VMEM),
        scratch_shapes=[
            pltpu.VMEM(populations.shape, bf16),
            pltpu.VMEM((2 * block, 128), f32),
            pltpu.VMEM((10, (tiles + 2) * size_x, 128), f32),
            pltpu.VMEM((5, tiles * size_x, 128), f32),
            pltpu.VMEM((38 * block, 128), f32),
            pltpu.VMEM((STEPS, 2, 2, tiles, 128), bf16),
            pltpu.VMEM((STEPS, 2, halves, 8, 128), bf16),
            pltpu.VMEM((STEPS, 2, 2, tiles, 128), bf16),
            pltpu.VMEM((STEPS, 2, halves, 8, 128), bf16),
            pltpu.VMEM((STEPS, 4, 8, 128), bf16),
            pltpu.VMEM((STEPS, 2, 10, tiles, 128), bf16),
            pltpu.VMEM((STEPS, 2, 5, halves, 8, 128), bf16),
            pltpu.VMEM((STEPS, 2, 10, tiles, 128), bf16),
            pltpu.VMEM((STEPS, 2, 5, halves, 8, 128), bf16),
            pltpu.VMEM((STEPS, 4, 8, 128), bf16),
            pltpu.SemaphoreType.DMA((tiles,)),
            pltpu.SemaphoreType.DMA((2 * STEPS, 8)),
            pltpu.SemaphoreType.DMA((2 * STEPS, 8)),
        ],
        compiler_params=pltpu.CompilerParams(
            collective_id=0, has_side_effects=True, vmem_limit_bytes=40 * 1024 * 1024
        ),
    )(populations, wall_class, planes)


def solution(mesh):
    in_specs = (P(None, None, "gx", "gy"), P("gx", "gy"), P())
    out_specs = P(None, None, "gx", "gy")
    return jax.shard_map(
        functools.partial(on_device, mesh.shape["gx"], mesh.shape["gy"]),
        mesh=mesh,
        in_specs=in_specs,
        out_specs=out_specs,
        check_vma=False,
    )
```

```python
import functools

import jax
import jax.numpy as jnp
import numpy as np
from jax import lax
from jax.experimental import pallas as pl
from jax.experimental.pallas import tpu as pltpu
from jax.sharding import PartitionSpec as P

NZ = 64
STEPS = 2
MESH = pl.DeviceIdType.MESH
velocities = (
    (0, 0, 0),
    (1, 0, 0),
    (-1, 0, 0),
    (0, 1, 0),
    (0, -1, 0),
    (0, 0, 1),
    (0, 0, -1),
    (1, 1, 0),
    (-1, -1, 0),
    (1, -1, 0),
    (-1, 1, 0),
    (1, 0, 1),
    (-1, 0, -1),
    (1, 0, -1),
    (-1, 0, 1),
    (0, 1, 1),
    (0, -1, -1),
    (0, 1, -1),
    (0, -1, 1),
)
lattice_weights = (1.0 / 3.0,) + (1.0 / 18.0,) * 6 + (1.0 / 36.0,) * 12
COUPLING = 2.5
RELAX_TIMES = (1.0, 0.8)
STRENGTHS = (0.0, 0.15, 0.35, 0.6)
INLET_DENSITY = (1.0, 0.03)
OUTLET_DENSITY = (0.03, 1.0)
along_x = ((1, 7, 9, 11, 13), (2, 8, 10, 12, 14))
along_y = ((3, 7, 10, 15, 17), (4, 8, 9, 16, 18))
along_edge = {(0, 0): 7, (1, 1): 8, (0, 1): 9, (1, 0): 10}
EDGES = ((0, 0), (0, 1), (1, 0), (1, 1))

HALO = 8


def opposite(direction):
    if direction == 0:
        return 0
    return direction + 1 if direction % 2 == 1 else direction - 1


def face_order(side, half, halves):
    edge = along_edge[0 if half == halves - 1 else 1, side]
    return (edge,) + tuple(d for d in along_y[side] if d != edge)


X_PARTS = 4 + 5 + 10
Y_PARTS = 2 + 3 + 5
EDGE_PARTS = 2 + 3 + 1


def kernel(
    nx_devices,
    ny_devices,
    pops_hbm,
    wall_hbm,
    planes_hbm,
    out_ref,
    pops,
    wall_ref,
    planes_ref,
    field,
    spread,
    aux,
    held_x,
    held_y,
    stream,
    send_x,
    send_y,
    recv_x,
    recv_y,
    recv_c,
    in_sem,
    send_sem,
    recv_sem,
):
    size_x = pops.shape[2]
    tiles = pops.shape[3] // 128
    halves = size_x // 8
    rows = size_x + 2 * HALO
    block = (tiles + 2) * rows
    first_row = HALO
    last_row = HALO + size_x - 1
    f32 = jnp.float32
    bf16 = jnp.bfloat16

    gx = lax.axis_index("gx")
    gy = lax.axis_index("gy")
    near_x = (lax.rem(gx + 1, nx_devices), lax.rem(gx + nx_devices - 1, nx_devices))
    near_y = (lax.rem(gy + 1, ny_devices), lax.rem(gy + ny_devices - 1, ny_devices))

    barrier = pltpu.get_barrier_semaphore()
    targets = [(near_x[0], gy), (near_x[1], gy), (gx, near_y[0]), (gx, near_y[1])]
    targets += [(near_x[i], near_y[j]) for i, j in EDGES]
    for target in targets:
        pl.semaphore_signal(barrier, inc=1, device_id=target, device_id_type=MESH)

    def load_in(t):
        lanes = pl.ds(pl.multiple_of(t * 128, 128), 128)
        return pltpu.make_async_copy(
            pops_hbm.at[:, :, :, lanes], pops.at[:, :, :, lanes], in_sem.at[t]
        )

    load_wall = pltpu.make_async_copy(wall_hbm, wall_ref, in_sem.at[tiles])
    load_planes = pltpu.make_async_copy(planes_hbm, planes_ref, in_sem.at[tiles + 1])
    load_wall.start()
    for t in range(tiles):
        load_in(t).start()
    load_planes.start()

    lane = lax.broadcasted_iota(jnp.int32, (8, 128), 1)
    row_index = lax.broadcasted_iota(jnp.int32, (8, 128), 0)
    low = lane < NZ
    first_z = jnp.logical_or(lane == 0, lane == NZ)
    last_z = jnp.logical_or(lane == NZ - 1, lane == 2 * NZ - 1)

    def roll(value, by):
        return pltpu.roll(value, by % 128, 1)

    def z_from_below(value, turned):
        return roll(jnp.where(last_z, turned, value), 1)

    def z_from_above(value, turned):
        return roll(jnp.where(first_z, turned, value), -1)

    def at(index, tile, row):
        return pl.ds(pl.multiple_of(index * block + tile * rows + row, 8), 8)

    def off(index, tile, row):
        return pl.ds(index * block + tile * rows + row, 8)

    def across(index, row, by=0):
        return pl.ds(index * block + (1 + by) * rows + row, tiles, stride=rows)

    def wall_at(t, half):
        lanes = pl.ds(pl.multiple_of(t * 128, 128), 128)
        return wall_ref[half * 8 : half * 8 + 8, lanes]

    def pop_at(component, direction, t, half):
        lanes = pl.ds(pl.multiple_of(t * 128, 128), 128)
        return pops[component, direction, half * 8 : half * 8 + 8, lanes].astype(f32)

    rates = [1.0 / value for value in RELAX_TIMES]
    gains = [-3.0 * value / (36.0 * COUPLING) for value in RELAX_TIMES]

    def store_potential(t, half, densities):
        wall = wall_at(t, half)
        fluid = wall == 0
        strength = jnp.where(
            wall == 1, STRENGTHS[1], jnp.where(wall == 2, STRENGTHS[2], STRENGTHS[3])
        )
        oil = COUPLING * (1.0 - jnp.exp(-densities[0]))
        brine = COUPLING * (1.0 - jnp.exp(-densities[1]))
        field[at(0, t + 1, HALO + half * 8), :] = jnp.where(fluid, brine, strength)
        field[at(1, t + 1, HALO + half * 8), :] = jnp.where(fluid, oil, -strength)
        aux[at(0, t + 1, HALO + half * 8), :] = densities[0]
        aux[at(1, t + 1, HALO + half * 8), :] = densities[1]

    def first_density(t, carry):
        load_in(t).wait()
        for half in range(halves):
            densities = []
            for component in range(2):
                total = pop_at(component, 0, t, half)
                for direction in range(1, 19):
                    total = total + pop_at(component, direction, t, half)
                densities.append(total)
            store_potential(t, half, densities)
        return carry

    def kept_part(component, fluid, own, bounced):
        kept = 1.0 - rates[component]
        return jnp.where(fluid, kept * own if kept != 0.0 else 0.0, bounced)

    def moments(t, carry):
        for half in range(halves):
            place = t + 1, HALO + half * 8
            fluid = wall_at(t, half) == 0
            side = 0 if half == halves - 1 else 1
            momenta = []
            for component in range(2):
                gap = [None] * 19
                for direction in range(1, 19, 2):
                    one = pop_at(component, direction, t, half)
                    two = pop_at(component, direction + 1, t, half)
                    gap[direction] = one - two
                    for toward, own, bounced in ((direction, one, two), (direction + 1, two, one)):
                        if toward in along_x[side]:
                            index = 5 * component + along_x[side].index(toward)
                            start = pl.multiple_of((index * tiles + t) * size_x + half * 8, 8)
                            held_x[pl.ds(start, 8), :] = kept_part(component, fluid, own, bounced)
                momenta.append(
                    (
                        (gap[1] + gap[7]) + (gap[9] + gap[11]) + gap[13],
                        (gap[3] + gap[7]) + (gap[15] - gap[9]) + gap[17],
                        (gap[5] + gap[11]) + (gap[15] - gap[13]) - gap[17],
                    )
                )
            densities = [aux[at(component, *place), :] for component in range(2)]
            inverse = 3.0 / (densities[0] * rates[0] + densities[1] * rates[1])
            for axis_pos in range(3):
                aux[at(2 + axis_pos, *place), :] = (
                    momenta[0][axis_pos] * rates[0] + momenta[1][axis_pos] * rates[1]
                ) * inverse
            for component in range(2):
                gain = gains[component] * field[at(1 - component, *place), :] / densities[component]
                aux[at(5 + component, *place), :] = jnp.where(fluid, gain, 0.0)
                aux[at(component, *place), :] = jnp.where(fluid, densities[component], 0.0)
        return carry

    def pack(side, one, two):
        turned = roll(two, NZ)
        return jnp.where(low, turned, one) if side == 0 else jnp.where(low, one, turned)

    def send_edges(step):
        for side in range(2):
            row, inner = (last_row, last_row - 1) if side == 0 else (first_row, first_row + 1)
            for index in range(2):
                send_x[step, side, index] = field[across(index, row), :].astype(bf16)
                send_x[step, side, 2 + index] = field[across(index, inner), :].astype(bf16)
            for index in range(5):
                send_x[step, side, 4 + index] = aux[across(index, row), :].astype(bf16)
            for index in range(10):
                start = index * tiles * size_x + row - HALO
                part = held_x[pl.ds(start, tiles, stride=size_x), :]
                send_x[step, side, 9 + index] = part.astype(bf16)
            t = tiles - 1 if side == 0 else 0
            for half in range(halves):
                place = t + 1, HALO + half * 8
                fluid = wall_at(t, half) == 0
                for index in range(2):
                    send_y[step, side, half, index] = field[at(index, *place), :].astype(bf16)
                for index, (one, two) in enumerate(((0, 1), (2, 3), (4, 4))):
                    packed = pack(side, aux[at(one, *place), :], aux[at(two, *place), :])
                    send_y[step, side, half, 2 + index] = packed.astype(bf16)
                for index, direction in enumerate(face_order(side, half, halves)):
                    parts = [
                        kept_part(
                            component,
                            fluid,
                            pop_at(component, direction, t, half),
                            pop_at(component, opposite(direction), t, half),
                        )
                        for component in range(2)
                    ]
                    send_y[step, side, half, 5 + index] = pack(side, *parts).astype(bf16)
        copies = []
        for place, (i, j) in enumerate(EDGES):
            source = send_y.at[step, j, halves - 1 if i == 0 else 0, pl.ds(0, EDGE_PARTS)]
            copies.append((source, recv_c.at[step, place], (near_x[i], near_y[j])))
        for side in range(2):
            copies.append((send_x.at[step, side], recv_x.at[step, side], (near_x[side], gy)))
            copies.append((send_y.at[step, side], recv_y.at[step, side], (gx, near_y[side])))
        started = []
        for place, (source, target, device) in enumerate(copies):
            copy = pltpu.make_async_remote_copy(
                src_ref=source,
                dst_ref=target,
                send_sem=send_sem.at[step, place],
                recv_sem=recv_sem.at[step, place],
                device_id=device,
                device_id_type=MESH,
            )
            copy.start()
            started.append(copy)
        return started

    def gain_of(component, source, density):
        return jnp.where(density == 0.0, 0.0, gains[component] * source / density)

    def receive_edges(step, copies):
        for copy in copies:
            copy.wait()
        for side in range(2):
            row, outer = (first_row - 1, first_row - 2) if side == 0 else (last_row + 1, last_row + 2)
            sources = []
            for index in range(2):
                source = recv_x[step, side, index].astype(f32)
                sources.append(source)
                field[across(index, row), :] = source
                field[across(index, outer), :] = recv_x[step, side, 2 + index].astype(f32)
            for index in range(5):
                value = recv_x[step, side, 4 + index].astype(f32)
                aux[across(index, row), :] = value
                if index < 2:
                    aux[across(5 + index, row), :] = gain_of(index, sources[1 - index], value)
            tile = 0 if side == 0 else tiles + 1

            def unpack(load, start, order):
                sources = [load(index) for index in range(2)]
                for index in range(2):
                    field[at(index, tile, start), :] = sources[index]
                for index, (one, two) in enumerate(((0, 1), (2, 3), (4, None))):
                    value = load(2 + index)
                    turned = roll(value, NZ)
                    aux[at(one, tile, start), :] = value
                    if two is not None:
                        aux[at(two, tile, start), :] = turned
                    if index == 0:
                        for component, density in ((0, value), (1, turned)):
                            gain = gain_of(component, sources[1 - component], density)
                            aux[at(5 + component, tile, start), :] = gain
                for index, direction in enumerate(order):
                    value = load(5 + index)
                    turned = roll(value, NZ)
                    place = along_y[side].index(direction)
                    for component, part in ((0, value), (1, turned)):
                        base = ((5 * component + place) * 2 + side) * rows
                        held_y[pl.ds(base + start, 8), :] = part

            for half in range(halves):
                unpack(
                    lambda index: recv_y[step, side, half, index].astype(f32),
                    HALO + half * 8,
                    face_order(side, half, halves),
                )
            for place, (i, j) in enumerate(EDGES):
                if j == side:
                    unpack(
                        lambda index: recv_c[step, place, index].astype(f32),
                        0 if i == 0 else HALO + size_x,
                        (along_edge[i, j],),
                    )

    windows = tuple(range(first_row - 1, last_row - 6, 8)) + (last_row - 6,)

    def spread_x(tile, carry):
        for start in windows:
            for index in range(2):
                centre = field[off(index, tile, start), :]
                above = field[off(index, tile, start + 1), :]
                below = field[off(index, tile, start - 1), :]
                gap = above - below
                total = 2.0 * centre + (above + below)
                spread[off(5 * index, tile, start), :] = gap
                spread[off(5 * index + 1, tile, start), :] = total
                spread[off(5 * index + 2, tile, start), :] = roll(gap, NZ)
                spread[off(5 * index + 3, tile, start), :] = roll(total, NZ)
                spread[off(5 * index + 4, tile, start), :] = roll(centre, NZ)
        return carry

    def pull_of(index, where):
        def held(kind, by=0):
            return spread[where(5 * index + kind, by), :]

        def upper(here, above):
            return jnp.where(low, here, above)

        def lower(here, below):
            return jnp.where(low, below, here)

        gap = held(0)
        turned_gap = held(2)
        pull_x = 2.0 * gap + (upper(turned_gap, held(2, 1)) + lower(turned_gap, held(2, -1)))
        pull_x = pull_x + (z_from_below(gap, turned_gap) + z_from_above(gap, turned_gap))
        turned_total = held(3)
        pull_y = upper(turned_total, held(3, 1)) - lower(turned_total, held(3, -1))
        turned = held(4)
        y_above = upper(turned, held(4, 1))
        y_below = lower(turned, held(4, -1))
        centre = field[where(index, 0), :]
        turned_y_above = jnp.where(low, field[where(index, 1), :], centre)
        turned_y_below = jnp.where(low, centre, field[where(index, -1), :])
        gap_y = y_above - y_below
        turned_gap_y = turned_y_above - turned_y_below
        pull_y = pull_y + (z_from_below(gap_y, turned_gap_y) + z_from_above(gap_y, turned_gap_y))
        plane = held(1) + (y_above + y_below)
        turned_plane = turned_total + (turned_y_above + turned_y_below)
        pull_z = z_from_above(plane, turned_plane) - z_from_below(plane, turned_plane)
        return pull_x, pull_y, pull_z

    def moved(direction, value):
        _, along, upward = velocities[direction]
        if along != 0 or upward != 0:
            turned = roll(value, NZ)
            if along != 0:
                value, turned = turned, value
            if upward == 1:
                value = z_from_below(value, turned)
            elif upward == -1:
                value = z_from_above(value, turned)
        return value

    def equilibria(component, where, directions):
        pull = pull_of(component, where)
        density = aux[where(component, 0), :]
        gain = aux[where(5 + component, 0), :]
        speed = [aux[where(2 + axis_pos, 0), :] + gain * pull[axis_pos] for axis_pos in range(3)]
        square = speed[0] * speed[0] + speed[1] * speed[1] + speed[2] * speed[2]
        level = 1.0 - square * (1.0 / 6.0)
        light = density * (rates[component] / 36.0)
        heavy = density * (rates[component] / 18.0)
        light_level = light * level
        heavy_level = heavy * level
        if 0 in directions:
            yield 0, 6.0 * heavy_level
        for direction in range(1, 19, 2):
            if direction not in directions and direction + 1 not in directions:
                continue
            along = None
            for axis_pos in range(3):
                part = velocities[direction][axis_pos]
                if part == 1:
                    along = speed[axis_pos] if along is None else along + speed[axis_pos]
                elif part == -1:
                    along = along - speed[axis_pos]
            weighted = (heavy if direction < 7 else light) * along
            even = (heavy_level if direction < 7 else light_level) + 0.5 * (weighted * along)
            if direction in directions:
                yield direction, even + weighted
            if direction + 1 in directions:
                yield direction + 1, even - weighted

    def collide(t, carry):
        for half in range(halves):
            fluid = wall_at(t, half) == 0

            def where(index, by):
                return at(index, t + 1 + by, HALO + half * 8)

            for component in range(2):
                kept = 1.0 - rates[component]
                for direction, relaxed in equilibria(component, where, range(19)):
                    if kept != 0.0:
                        relaxed = relaxed + kept * pop_at(component, direction, t, half)
                    bounced = pop_at(component, opposite(direction), t, half)
                    value = moved(direction, jnp.where(fluid, relaxed, bounced))
                    stream[where(19 * component + direction, 0), :] = value
        return carry

    def collide_outside(step):
        for side in range(2):
            row = first_row - 1 if side == 0 else last_row + 1
            for component in range(2):

                def where(index, by):
                    return across(index, row, by)

                for direction, relaxed in equilibria(component, where, along_x[side]):
                    place = 5 * component + along_x[side].index(direction)
                    value = relaxed + recv_x[step, side, 9 + place].astype(f32)
                    stream[where(19 * component + direction, 0), :] = moved(direction, value)
            tile = 0 if side == 0 else tiles + 1
            for start in windows:
                for component in range(2):

                    def where(index, by):
                        return off(index, min(max(tile + by, 0), tiles + 1), start)

                    for direction, relaxed in equilibria(component, where, along_y[side]):
                        place = 5 * component + along_y[side].index(direction)
                        part = held_y[pl.ds((place * 2 + side) * rows + start, 8), :]
                        value = moved(direction, relaxed + part)
                        stream[where(19 * component + direction, 0), :] = value

    def settle_step(last):
        target = out_ref if last else pops

        def read(t, carry):
            lanes = pl.ds(pl.multiple_of(t * 128, 128), 128)
            for half in range(halves):
                fluid = wall_at(t, half) == 0
                xglobal = gx * size_x + half * 8 + row_index
                inlet = jnp.logical_and(xglobal == planes_ref[0], fluid)
                outlet = jnp.logical_and(xglobal == planes_ref[1], fluid)
                fixed = jnp.logical_or(inlet, outlet)
                densities = []
                for component in range(2):
                    forced = {}
                    for weight in sorted(set(lattice_weights)):
                        values = [
                            float(np.asarray(weight * level[component], jnp.bfloat16))
                            for level in (INLET_DENSITY, OUTLET_DENSITY)
                        ]
                        forced[weight] = jnp.where(inlet, values[0], values[1])
                    total = None
                    for direction in range(19):
                        step_x, step_y, _ = velocities[direction]
                        index = 19 * component + direction
                        start = HALO + half * 8 - step_x
                        value = stream[off(index, t + 1, start), :]
                        if step_y == 1:
                            value = jnp.where(low, stream[off(index, t, start), :], value)
                        elif step_y == -1:
                            value = jnp.where(low, value, stream[off(index, t + 2, start), :])
                        value = jnp.where(fixed, forced[lattice_weights[direction]], value)
                        narrow = value.astype(bf16)
                        target[component, direction, half * 8 : half * 8 + 8, lanes] = narrow
                        if not last:
                            wide = narrow.astype(f32)
                            total = wide if total is None else total + wide
                    densities.append(total)
                if not last:
                    store_potential(t, half, densities)
            return carry

        lax.fori_loop(0, tiles, read, 0)

    load_wall.wait()
    lax.fori_loop(0, tiles, first_density, 0)
    load_planes.wait()
    lax.fori_loop(0, tiles, moments, 0)
    pl.semaphore_wait(barrier, len(targets))
    for step in range(STEPS):
        if step > 0:
            lax.fori_loop(0, tiles, moments, 0)
        copies = send_edges(step)
        receive_edges(step, copies)
        lax.fori_loop(0, tiles + 2, spread_x, 0)
        collide_outside(step)
        lax.fori_loop(0, tiles, collide, 0)
        settle_step(step == STEPS - 1)


def on_device(nx_devices, ny_devices, populations, wall_class, planes):
    size_x, width = populations.shape[2:]
    tiles = width // 128
    halves = size_x // 8
    rows = size_x + 2 * HALO
    block = (tiles + 2) * rows
    bf16 = jnp.bfloat16
    f32 = jnp.float32
    return pl.pallas_call(
        functools.partial(kernel, nx_devices, ny_devices),
        out_shape=jax.ShapeDtypeStruct(populations.shape, bf16),
        in_specs=[pl.BlockSpec(memory_space=pltpu.HBM)] * 3,
        out_specs=pl.BlockSpec(memory_space=pltpu.VMEM),
        scratch_shapes=[
            pltpu.VMEM(populations.shape, bf16),
            pltpu.VMEM(wall_class.shape, wall_class.dtype),
            pltpu.SMEM(planes.shape, planes.dtype),
            pltpu.VMEM((2 * block, 128), f32),
            pltpu.VMEM((10 * block, 128), f32),
            pltpu.VMEM((7 * block, 128), f32),
            pltpu.VMEM((10 * tiles * size_x, 128), f32),
            pltpu.VMEM((20 * rows, 128), f32),
            pltpu.VMEM((38 * block, 128), f32),
            pltpu.VMEM((STEPS, 2, X_PARTS, tiles, 128), bf16),
            pltpu.VMEM((STEPS, 2, halves, Y_PARTS, 8, 128), bf16),
            pltpu.VMEM((STEPS, 2, X_PARTS, tiles, 128), bf16),
            pltpu.VMEM((STEPS, 2, halves, Y_PARTS, 8, 128), bf16),
            pltpu.VMEM((STEPS, 4, EDGE_PARTS, 8, 128), bf16),
            pltpu.SemaphoreType.DMA((tiles + 2,)),
            pltpu.SemaphoreType.DMA((STEPS, 8)),
            pltpu.SemaphoreType.DMA((STEPS, 8)),
        ],
        compiler_params=pltpu.CompilerParams(
            collective_id=0, has_side_effects=True, vmem_limit_bytes=40 * 1024 * 1024
        ),
    )(*[pltpu.with_memory_space_constraint(v, pltpu.HBM) for v in (populations, wall_class, planes)])


def solution(mesh):
    in_specs = (P(None, None, "gx", "gy"), P("gx", "gy"), P())
    out_specs = P(None, None, "gx", "gy")
    return jax.shard_map(
        functools.partial(on_device, mesh.shape["gx"], mesh.shape["gy"]),
        mesh=mesh,
        in_specs=in_specs,
        out_specs=out_specs,
        check_vma=False,
    )
```

```python
import functools

import jax
import jax.numpy as jnp
import numpy as np
from jax import lax
from jax.experimental import pallas as pl
from jax.experimental.pallas import tpu as pltpu
from jax.sharding import PartitionSpec as P

NZ = 64
STEPS = 2
MESH = pl.DeviceIdType.MESH
velocities = (
    (0, 0, 0),
    (1, 0, 0),
    (-1, 0, 0),
    (0, 1, 0),
    (0, -1, 0),
    (0, 0, 1),
    (0, 0, -1),
    (1, 1, 0),
    (-1, -1, 0),
    (1, -1, 0),
    (-1, 1, 0),
    (1, 0, 1),
    (-1, 0, -1),
    (1, 0, -1),
    (-1, 0, 1),
    (0, 1, 1),
    (0, -1, -1),
    (0, 1, -1),
    (0, -1, 1),
)
lattice_weights = (1.0 / 3.0,) + (1.0 / 18.0,) * 6 + (1.0 / 36.0,) * 12
COUPLING = 2.5
RELAX_TIMES = (1.0, 0.8)
STRENGTHS = (0.0, 0.15, 0.35, 0.6)
INLET_DENSITY = (1.0, 0.03)
OUTLET_DENSITY = (0.03, 1.0)
along_x = ((1, 7, 9, 11, 13), (2, 8, 10, 12, 14))
along_y = ((3, 7, 10, 15, 17), (4, 8, 9, 16, 18))
along_edge = {(0, 0): 7, (1, 1): 8, (0, 1): 9, (1, 0): 10}
EDGES = ((0, 0), (0, 1), (1, 0), (1, 1))

HALO = 8


def opposite(direction):
    if direction == 0:
        return 0
    return direction + 1 if direction % 2 == 1 else direction - 1


def face_order(side, half, halves):
    edge = along_edge[0 if half == halves - 1 else 1, side]
    return (edge,) + tuple(d for d in along_y[side] if d != edge)


X_PARTS = 4 + 5 + 10
Y_PARTS = 2 + 3 + 5
EDGE_PARTS = 2 + 3 + 1


def kernel(
    nx_devices,
    ny_devices,
    pops_hbm,
    wall_hbm,
    planes_hbm,
    out_ref,
    pops,
    wall_ref,
    planes_ref,
    field,
    spread,
    aux,
    held_x,
    held_y,
    stream,
    send_x,
    send_y,
    recv_x,
    recv_y,
    recv_c,
    in_sem,
    send_sem,
    recv_sem,
):
    size_x = pops.shape[2]
    tiles = pops.shape[3] // 128
    halves = size_x // 8
    rows = size_x + 2 * HALO
    block = (tiles + 2) * rows
    first_row = HALO
    last_row = HALO + size_x - 1
    f32 = jnp.float32
    bf16 = jnp.bfloat16

    gx = lax.axis_index("gx")
    gy = lax.axis_index("gy")
    near_x = (lax.rem(gx + 1, nx_devices), lax.rem(gx + nx_devices - 1, nx_devices))
    near_y = (lax.rem(gy + 1, ny_devices), lax.rem(gy + ny_devices - 1, ny_devices))

    barrier = pltpu.get_barrier_semaphore()
    targets = [(near_x[0], gy), (near_x[1], gy), (gx, near_y[0]), (gx, near_y[1])]
    targets += [(near_x[i], near_y[j]) for i, j in EDGES]
    for target in targets:
        pl.semaphore_signal(barrier, inc=1, device_id=target, device_id_type=MESH)

    def load_in(t):
        lanes = pl.ds(pl.multiple_of(t * 128, 128), 128)
        return pltpu.make_async_copy(
            pops_hbm.at[:, :, :, lanes], pops.at[:, :, :, lanes], in_sem.at[t]
        )

    load_wall = pltpu.make_async_copy(wall_hbm, wall_ref, in_sem.at[tiles])
    load_planes = pltpu.make_async_copy(planes_hbm, planes_ref, in_sem.at[tiles + 1])
    load_wall.start()
    for t in range(tiles):
        load_in(t).start()
    load_planes.start()

    lane = lax.broadcasted_iota(jnp.int32, (8, 128), 1)
    row_index = lax.broadcasted_iota(jnp.int32, (8, 128), 0)
    low = lane < NZ
    first_z = jnp.logical_or(lane == 0, lane == NZ)
    last_z = jnp.logical_or(lane == NZ - 1, lane == 2 * NZ - 1)

    def roll(value, by):
        return pltpu.roll(value, by % 128, 1)

    def z_from_below(value, turned):
        return roll(jnp.where(last_z, turned, value), 1)

    def z_from_above(value, turned):
        return roll(jnp.where(first_z, turned, value), -1)

    def at(index, tile, row):
        return pl.ds(pl.multiple_of(index * block + tile * rows + row, 8), 8)

    def off(index, tile, row):
        return pl.ds(index * block + tile * rows + row, 8)

    def across(index, row, by=0):
        return pl.ds(index * block + (1 + by) * rows + row, tiles, stride=rows)

    def wall_at(t, half):
        lanes = pl.ds(pl.multiple_of(t * 128, 128), 128)
        return wall_ref[half * 8 : half * 8 + 8, lanes]

    def pop_at(component, direction, t, half):
        lanes = pl.ds(pl.multiple_of(t * 128, 128), 128)
        return pops[component, direction, half * 8 : half * 8 + 8, lanes].astype(f32)

    rates = [1.0 / value for value in RELAX_TIMES]
    gains = [-3.0 * value / (36.0 * COUPLING) for value in RELAX_TIMES]

    def kept_part(component, fluid, own, bounced):
        kept = 1.0 - rates[component]
        return jnp.where(fluid, kept * own if kept != 0.0 else 0.0, bounced)

    def absorb(t, half, get):
        place = t + 1, HALO + half * 8
        wall = wall_at(t, half)
        fluid = wall == 0
        side = 0 if half == halves - 1 else 1
        densities, momenta = [], []
        for component in range(2):
            total = get(component, 0)
            parts = [None] * 3
            for direction in range(1, 19, 2):
                one, two = get(component, direction), get(component, direction + 1)
                total = total + (one + two)
                gap = one - two
                for axis_pos in range(3):
                    along = velocities[direction][axis_pos]
                    if along != 0:
                        if parts[axis_pos] is None:
                            parts[axis_pos] = gap
                        else:
                            parts[axis_pos] = parts[axis_pos] + gap if along == 1 else parts[axis_pos] - gap
                for toward, own, bounced in ((direction, one, two), (direction + 1, two, one)):
                    if toward in along_x[side]:
                        index = 5 * component + along_x[side].index(toward)
                        start = pl.multiple_of((index * tiles + t) * size_x + half * 8, 8)
                        held_x[pl.ds(start, 8), :] = kept_part(component, fluid, own, bounced)
            densities.append(total)
            momenta.append(parts)
        strength = jnp.where(
            wall == 1, STRENGTHS[1], jnp.where(wall == 2, STRENGTHS[2], STRENGTHS[3])
        )
        pushes = [COUPLING * (1.0 - jnp.exp(-densities[component])) for component in range(2)]
        field[at(0, *place), :] = jnp.where(fluid, pushes[1], strength)
        field[at(1, *place), :] = jnp.where(fluid, pushes[0], -strength)
        inverse = 3.0 / (densities[0] * rates[0] + densities[1] * rates[1])
        for axis_pos in range(3):
            aux[at(2 + axis_pos, *place), :] = (
                momenta[0][axis_pos] * rates[0] + momenta[1][axis_pos] * rates[1]
            ) * inverse
        for component in range(2):
            gain = gains[component] * pushes[component] / densities[component]
            aux[at(5 + component, *place), :] = jnp.where(fluid, gain, 0.0)
            aux[at(component, *place), :] = jnp.where(fluid, densities[component], 0.0)

    def first_absorb(t, carry):
        load_in(t).wait()
        for half in range(halves):
            absorb(t, half, lambda component, direction: pop_at(component, direction, t, half))
        return carry

    def pack(side, one, two):
        turned = roll(two, NZ)
        return jnp.where(low, turned, one) if side == 0 else jnp.where(low, one, turned)

    def send_edges(step):
        for side in range(2):
            row, inner = (last_row, last_row - 1) if side == 0 else (first_row, first_row + 1)
            for index in range(2):
                send_x[step, side, index] = field[across(index, row), :].astype(bf16)
                send_x[step, side, 2 + index] = field[across(index, inner), :].astype(bf16)
            for index in range(5):
                send_x[step, side, 4 + index] = aux[across(index, row), :].astype(bf16)
            for index in range(10):
                start = index * tiles * size_x + row - HALO
                part = held_x[pl.ds(start, tiles, stride=size_x), :]
                send_x[step, side, 9 + index] = part.astype(bf16)
            t = tiles - 1 if side == 0 else 0
            for half in range(halves):
                place = t + 1, HALO + half * 8
                fluid = wall_at(t, half) == 0
                for index in range(2):
                    send_y[step, side, half, index] = field[at(index, *place), :].astype(bf16)
                for index, (one, two) in enumerate(((0, 1), (2, 3), (4, 4))):
                    packed = pack(side, aux[at(one, *place), :], aux[at(two, *place), :])
                    send_y[step, side, half, 2 + index] = packed.astype(bf16)
                for index, direction in enumerate(face_order(side, half, halves)):
                    parts = [
                        kept_part(
                            component,
                            fluid,
                            pop_at(component, direction, t, half),
                            pop_at(component, opposite(direction), t, half),
                        )
                        for component in range(2)
                    ]
                    send_y[step, side, half, 5 + index] = pack(side, *parts).astype(bf16)
        copies = []
        for place, (i, j) in enumerate(EDGES):
            source = send_y.at[step, j, halves - 1 if i == 0 else 0, pl.ds(0, EDGE_PARTS)]
            copies.append((source, recv_c.at[step, place], (near_x[i], near_y[j])))
        for side in range(2):
            copies.append((send_x.at[step, side], recv_x.at[step, side], (near_x[side], gy)))
            copies.append((send_y.at[step, side], recv_y.at[step, side], (gx, near_y[side])))
        started = []
        for place, (source, target, device) in enumerate(copies):
            copy = pltpu.make_async_remote_copy(
                src_ref=source,
                dst_ref=target,
                send_sem=send_sem.at[step, place],
                recv_sem=recv_sem.at[step, place],
                device_id=device,
                device_id_type=MESH,
            )
            copy.start()
            started.append(copy)
        return started

    def gain_of(component, source, density):
        return jnp.where(density == 0.0, 0.0, gains[component] * source / density)

    def unpack_x(step, side):
        row, outer = (first_row - 1, first_row - 2) if side == 0 else (last_row + 1, last_row + 2)
        sources = []
        for index in range(2):
            source = recv_x[step, side, index].astype(f32)
            sources.append(source)
            field[across(index, row), :] = source
            field[across(index, outer), :] = recv_x[step, side, 2 + index].astype(f32)
        for index in range(5):
            value = recv_x[step, side, 4 + index].astype(f32)
            aux[across(index, row), :] = value
            if index < 2:
                aux[across(5 + index, row), :] = gain_of(index, sources[1 - index], value)

    def unpack_y(side, load, start, order):
        tile = 0 if side == 0 else tiles + 1
        sources = [load(index) for index in range(2)]
        for index in range(2):
            field[at(index, tile, start), :] = sources[index]
        for index, (one, two) in enumerate(((0, 1), (2, 3), (4, None))):
            value = load(2 + index)
            turned = roll(value, NZ)
            aux[at(one, tile, start), :] = value
            if two is not None:
                aux[at(two, tile, start), :] = turned
            if index == 0:
                for component, density in ((0, value), (1, turned)):
                    gain = gain_of(component, sources[1 - component], density)
                    aux[at(5 + component, tile, start), :] = gain
        for index, direction in enumerate(order):
            value = load(5 + index)
            turned = roll(value, NZ)
            place = along_y[side].index(direction)
            for component, part in ((0, value), (1, turned)):
                base = ((5 * component + place) * 2 + side) * rows
                held_y[pl.ds(base + start, 8), :] = part

    def receive_faces(step, copies):
        for copy in copies[len(EDGES) :]:
            copy.wait_recv()
        for side in range(2):
            unpack_x(step, side)
            for half in range(halves):
                unpack_y(
                    side,
                    lambda index: recv_y[step, side, half, index].astype(f32),
                    HALO + half * 8,
                    face_order(side, half, halves),
                )

    def receive_corners(step, copies):
        for copy in copies[: len(EDGES)]:
            copy.wait_recv()
        for place, (i, j) in enumerate(EDGES):
            unpack_y(
                j,
                lambda index: recv_c[step, place, index].astype(f32),
                0 if i == 0 else HALO + size_x,
                (along_edge[i, j],),
            )

    inner_windows = tuple(range(first_row, last_row, 8))
    outer_windows = (first_row - 1, last_row - 6)
    middle_windows = tuple(range(first_row + 7, last_row - 6, 8))

    def spread_at(where):
        for index in range(2):
            centre = field[where(index, 0), :]
            above = field[where(index, 1), :]
            below = field[where(index, -1), :]
            gap = above - below
            total = 2.0 * centre + (above + below)
            spread[where(5 * index, 0), :] = gap
            spread[where(5 * index + 1, 0), :] = total
            spread[where(5 * index + 2, 0), :] = roll(gap, NZ)
            spread[where(5 * index + 3, 0), :] = roll(total, NZ)
            spread[where(5 * index + 4, 0), :] = roll(centre, NZ)

    def spread_tile(tile, starts):
        for start in starts:
            spread_at(lambda index, by: off(index, tile, start + by))

    def spread_row(row):
        spread_at(lambda index, by: across(index, row + by))

    def pull_of(index, where):
        def held(kind, by=0):
            return spread[where(5 * index + kind, by), :]

        def upper(here, above):
            return jnp.where(low, here, above)

        def lower(here, below):
            return jnp.where(low, below, here)

        gap = held(0)
        turned_gap = held(2)
        pull_x = 2.0 * gap + (upper(turned_gap, held(2, 1)) + lower(turned_gap, held(2, -1)))
        pull_x = pull_x + (z_from_below(gap, turned_gap) + z_from_above(gap, turned_gap))
        turned_total = held(3)
        pull_y = upper(turned_total, held(3, 1)) - lower(turned_total, held(3, -1))
        turned = held(4)
        y_above = upper(turned, held(4, 1))
        y_below = lower(turned, held(4, -1))
        centre = field[where(index, 0), :]
        turned_y_above = jnp.where(low, field[where(index, 1), :], centre)
        turned_y_below = jnp.where(low, centre, field[where(index, -1), :])
        gap_y = y_above - y_below
        turned_gap_y = turned_y_above - turned_y_below
        pull_y = pull_y + (z_from_below(gap_y, turned_gap_y) + z_from_above(gap_y, turned_gap_y))
        plane = held(1) + (y_above + y_below)
        turned_plane = turned_total + (turned_y_above + turned_y_below)
        pull_z = z_from_above(plane, turned_plane) - z_from_below(plane, turned_plane)
        return pull_x, pull_y, pull_z

    def moved(direction, value):
        _, along, upward = velocities[direction]
        if along != 0 or upward != 0:
            turned = roll(value, NZ)
            if along != 0:
                value, turned = turned, value
            if upward == 1:
                value = z_from_below(value, turned)
            elif upward == -1:
                value = z_from_above(value, turned)
        return value

    def equilibria(component, where, directions, left_out=None):
        pull = pull_of(component, where)
        density = aux[where(component, 0), :]
        if left_out is not None:
            density = jnp.where(left_out, 0.0, density)
        gain = aux[where(5 + component, 0), :]
        speed = [aux[where(2 + axis_pos, 0), :] + gain * pull[axis_pos] for axis_pos in range(3)]
        square = speed[0] * speed[0] + speed[1] * speed[1] + speed[2] * speed[2]
        level = 1.0 - square * (1.0 / 6.0)
        light = density * (rates[component] / 36.0)
        heavy = density * (rates[component] / 18.0)
        light_level = light * level
        heavy_level = heavy * level
        if 0 in directions:
            yield 0, 6.0 * heavy_level
        for direction in range(1, 19, 2):
            if direction not in directions and direction + 1 not in directions:
                continue
            along = None
            for axis_pos in range(3):
                part = velocities[direction][axis_pos]
                if part == 1:
                    along = speed[axis_pos] if along is None else along + speed[axis_pos]
                elif part == -1:
                    along = along - speed[axis_pos]
            weighted = (heavy if direction < 7 else light) * along
            even = (heavy_level if direction < 7 else light_level) + 0.5 * (weighted * along)
            if direction in directions:
                yield direction, even + weighted
            if direction + 1 in directions:
                yield direction + 1, even - weighted

    def collide(t):
        for half in range(halves):
            fluid = wall_at(t, half) == 0
            left_out = row_index == (7 if half == halves - 1 else 0)

            def where(index, by):
                return at(index, t + 1 + by, HALO + half * 8)

            for component in range(2):
                kept = 1.0 - rates[component]
                for direction, relaxed in equilibria(component, where, range(19), left_out):
                    if kept != 0.0:
                        relaxed = relaxed + kept * pop_at(component, direction, t, half)
                    bounced = pop_at(component, opposite(direction), t, half)
                    value = moved(direction, jnp.where(fluid, relaxed, bounced))
                    stream[where(19 * component + direction, 0), :] = value

    def collide_row(row):
        for component in range(2):

            def where(index, by):
                return across(index, row, by)

            for direction, relaxed in equilibria(component, where, range(19)):
                place = where(19 * component + direction, 0)
                stream[place, :] = stream[place, :] + moved(direction, relaxed)

    def collide_outside_x(step, side):
        row = first_row - 1 if side == 0 else last_row + 1
        for component in range(2):

            def where(index, by):
                return across(index, row, by)

            for direction, relaxed in equilibria(component, where, along_x[side]):
                place = 5 * component + along_x[side].index(direction)
                value = relaxed + recv_x[step, side, 9 + place].astype(f32)
                stream[where(19 * component + direction, 0), :] = moved(direction, value)

    def collide_outside_y(side, starts):
        tile = 0 if side == 0 else tiles + 1
        for start in starts:
            for component in range(2):

                def where(index, by):
                    return off(index, min(max(tile + by, 0), tiles + 1), start)

                for direction, relaxed in equilibria(component, where, along_y[side]):
                    place = 5 * component + along_y[side].index(direction)
                    part = held_y[pl.ds((place * 2 + side) * rows + start, 8), :]
                    value = moved(direction, relaxed + part)
                    stream[where(19 * component + direction, 0), :] = value

    def settle_step(last):
        target = out_ref if last else pops

        def read(t, carry):
            lanes = pl.ds(pl.multiple_of(t * 128, 128), 128)
            for half in range(halves):
                fluid = wall_at(t, half) == 0
                xglobal = gx * size_x + half * 8 + row_index
                inlet = jnp.logical_and(xglobal == planes_ref[0], fluid)
                outlet = jnp.logical_and(xglobal == planes_ref[1], fluid)
                fixed = jnp.logical_or(inlet, outlet)
                forced = [{}, {}]
                for component in range(2):
                    for weight in sorted(set(lattice_weights)):
                        values = [
                            float(np.asarray(weight * level[component], bf16))
                            for level in (INLET_DENSITY, OUTLET_DENSITY)
                        ]
                        forced[component][weight] = jnp.where(inlet, values[0], values[1])

                def get(component, direction):
                    step_x, step_y, _ = velocities[direction]
                    index = 19 * component + direction
                    start = HALO + half * 8 - step_x
                    value = stream[off(index, t + 1, start), :]
                    if step_y == 1:
                        value = jnp.where(low, stream[off(index, t, start), :], value)
                    elif step_y == -1:
                        value = jnp.where(low, value, stream[off(index, t + 2, start), :])
                    value = jnp.where(fixed, forced[component][lattice_weights[direction]], value)
                    narrow = value.astype(bf16)
                    target[component, direction, half * 8 : half * 8 + 8, lanes] = narrow
                    return narrow.astype(f32)

                if last:
                    for component in range(2):
                        for direction in range(19):
                            get(component, direction)
                else:
                    absorb(t, half, get)
            return carry

        lax.fori_loop(0, tiles, read, 0)

    def clear(tile, carry):
        for index in range(2):
            for start in (0, HALO + size_x):
                field[at(index, tile, start), :] = jnp.zeros((8, 128), f32)
        return carry

    def each_tile(first, last, step, work):
        def body(k, carry):
            work(first + k * step)
            return carry

        lax.fori_loop(0, (last - first) // step + 1, body, 0)

    lax.fori_loop(0, tiles + 2, clear, 0)
    load_wall.wait()
    lax.fori_loop(0, tiles, first_absorb, 0)
    load_planes.wait()
    pl.semaphore_wait(barrier, len(targets))
    sent = []
    for step in range(STEPS):
        copies = send_edges(step)
        sent += copies
        each_tile(1, tiles, 1, lambda tile: spread_tile(tile, inner_windows))
        each_tile(1, tiles - 2, 1, collide)
        receive_faces(step, copies)
        for row in (first_row - 1, first_row, last_row, last_row + 1):
            spread_row(row)
        each_tile(0, tiles + 1, tiles + 1, lambda tile: spread_tile(tile, inner_windows))
        each_tile(0, tiles - 1, tiles - 1, collide)
        for side in range(2):
            collide_outside_y(side, middle_windows)
        receive_corners(step, copies)
        each_tile(0, tiles + 1, tiles + 1, lambda tile: spread_tile(tile, outer_windows))
        for side in range(2):
            collide_outside_y(side, outer_windows)
            collide_outside_x(step, side)
        each_tile(first_row, last_row, last_row - first_row, collide_row)
        settle_step(step == STEPS - 1)
    for copy in sent:
        copy.wait_send()


def on_device(nx_devices, ny_devices, populations, wall_class, planes):
    size_x, width = populations.shape[2:]
    tiles = width // 128
    halves = size_x // 8
    rows = size_x + 2 * HALO
    block = (tiles + 2) * rows
    bf16 = jnp.bfloat16
    f32 = jnp.float32
    return pl.pallas_call(
        functools.partial(kernel, nx_devices, ny_devices),
        out_shape=jax.ShapeDtypeStruct(populations.shape, bf16),
        in_specs=[pl.BlockSpec(memory_space=pltpu.HBM)] * 3,
        out_specs=pl.BlockSpec(memory_space=pltpu.VMEM),
        scratch_shapes=[
            pltpu.VMEM(populations.shape, bf16),
            pltpu.VMEM(wall_class.shape, wall_class.dtype),
            pltpu.SMEM(planes.shape, planes.dtype),
            pltpu.VMEM((2 * block, 128), f32),
            pltpu.VMEM((10 * block, 128), f32),
            pltpu.VMEM((7 * block, 128), f32),
            pltpu.VMEM((10 * tiles * size_x, 128), f32),
            pltpu.VMEM((20 * rows, 128), f32),
            pltpu.VMEM((38 * block, 128), f32),
            pltpu.VMEM((STEPS, 2, X_PARTS, tiles, 128), bf16),
            pltpu.VMEM((STEPS, 2, halves, Y_PARTS, 8, 128), bf16),
            pltpu.VMEM((STEPS, 2, X_PARTS, tiles, 128), bf16),
            pltpu.VMEM((STEPS, 2, halves, Y_PARTS, 8, 128), bf16),
            pltpu.VMEM((STEPS, 4, EDGE_PARTS, 8, 128), bf16),
            pltpu.SemaphoreType.DMA((tiles + 2,)),
            pltpu.SemaphoreType.DMA((STEPS, 8)),
            pltpu.SemaphoreType.DMA((STEPS, 8)),
        ],
        compiler_params=pltpu.CompilerParams(
            collective_id=0, has_side_effects=True, vmem_limit_bytes=40 * 1024 * 1024
        ),
    )(*[pltpu.with_memory_space_constraint(v, pltpu.HBM) for v in (populations, wall_class, planes)])


def solution(mesh):
    in_specs = (P(None, None, "gx", "gy"), P("gx", "gy"), P())
    out_specs = P(None, None, "gx", "gy")
    return jax.shard_map(
        functools.partial(on_device, mesh.shape["gx"], mesh.shape["gy"]),
        mesh=mesh,
        in_specs=in_specs,
        out_specs=out_specs,
        check_vma=False,
    )
```

```python
import functools

import jax
import jax.numpy as jnp
import numpy as np
from jax import lax
from jax.experimental import pallas as pl
from jax.experimental.pallas import tpu as pltpu
from jax.sharding import PartitionSpec as P

NZ = 64
STEPS = 2
MESH = pl.DeviceIdType.MESH
velocities = (
    (0, 0, 0),
    (1, 0, 0),
    (-1, 0, 0),
    (0, 1, 0),
    (0, -1, 0),
    (0, 0, 1),
    (0, 0, -1),
    (1, 1, 0),
    (-1, -1, 0),
    (1, -1, 0),
    (-1, 1, 0),
    (1, 0, 1),
    (-1, 0, -1),
    (1, 0, -1),
    (-1, 0, 1),
    (0, 1, 1),
    (0, -1, -1),
    (0, 1, -1),
    (0, -1, 1),
)
lattice_weights = (1.0 / 3.0,) + (1.0 / 18.0,) * 6 + (1.0 / 36.0,) * 12
COUPLING = 2.5
RELAX_TIMES = (1.0, 0.8)
STRENGTHS = (0.0, 0.15, 0.35, 0.6)
INLET_DENSITY = (1.0, 0.03)
OUTLET_DENSITY = (0.03, 1.0)
along_x = ((1, 7, 9, 11, 13), (2, 8, 10, 12, 14))
along_y = ((3, 7, 10, 15, 17), (4, 8, 9, 16, 18))
along_edge = {(0, 0): 7, (1, 1): 8, (0, 1): 9, (1, 0): 10}
EDGES = ((0, 0), (0, 1), (1, 0), (1, 1))

HALO = 8
SPARE = 8


def opposite(direction):
    if direction == 0:
        return 0
    return direction + 1 if direction % 2 == 1 else direction - 1


def face_order(side, half, halves):
    edge = along_edge[0 if half == halves - 1 else 1, side]
    return (edge,) + tuple(d for d in along_y[side] if d != edge)


X_PARTS = 4 + 5 + 10
Y_PARTS = 2 + 3 + 5
EDGE_PARTS = 2 + 3 + 1


def kernel(
    nx_devices,
    ny_devices,
    pops_hbm,
    wall_hbm,
    planes_hbm,
    out_ref,
    pops,
    wall_ref,
    planes_ref,
    field,
    spread,
    aux,
    held_x,
    held_y,
    stream,
    send_x,
    send_y,
    recv_x,
    recv_y,
    recv_c,
    in_sem,
    send_sem,
    recv_sem,
):
    size_x = pops.shape[2]
    tiles = pops.shape[3] // 128
    halves = size_x // 8
    rows = size_x + 2 * HALO + SPARE
    block = (tiles + 2) * rows
    first_row = HALO
    last_row = HALO + size_x - 1
    f32 = jnp.float32
    bf16 = jnp.bfloat16

    gx = lax.axis_index("gx")
    gy = lax.axis_index("gy")
    near_x = (lax.rem(gx + 1, nx_devices), lax.rem(gx + nx_devices - 1, nx_devices))
    near_y = (lax.rem(gy + 1, ny_devices), lax.rem(gy + ny_devices - 1, ny_devices))

    barrier = pltpu.get_barrier_semaphore()
    targets = [(near_x[i], near_y[j]) for i, j in EDGES]
    targets += [(near_x[0], gy), (near_x[1], gy), (gx, near_y[0]), (gx, near_y[1])]
    for target in targets:
        pl.semaphore_signal(barrier, inc=1, device_id=target, device_id_type=MESH)

    def load_in(t):
        lanes = pl.ds(pl.multiple_of(t * 128, 128), 128)
        return pltpu.make_async_copy(
            pops_hbm.at[:, :, :, lanes], pops.at[:, :, :, lanes], in_sem.at[t]
        )

    load_wall = pltpu.make_async_copy(wall_hbm, wall_ref, in_sem.at[tiles])
    load_planes = pltpu.make_async_copy(planes_hbm, planes_ref, in_sem.at[tiles + 1])
    load_wall.start()
    for t in range(tiles):
        load_in(t).start()
    load_planes.start()

    lane = lax.broadcasted_iota(jnp.int32, (8, 128), 1)
    row_index = lax.broadcasted_iota(jnp.int32, (8, 128), 0)
    low = lane < NZ
    first_z = jnp.logical_or(lane == 0, lane == NZ)
    last_z = jnp.logical_or(lane == NZ - 1, lane == 2 * NZ - 1)

    def roll(value, by):
        return pltpu.roll(value, by % 128, 1)

    def z_from_below(value, turned):
        return roll(jnp.where(last_z, turned, value), 1)

    def z_from_above(value, turned):
        return roll(jnp.where(first_z, turned, value), -1)

    def at(index, tile, row):
        return pl.ds(pl.multiple_of(index * block + tile * rows + row, 8), 8)

    def off(index, tile, row):
        return pl.ds(index * block + tile * rows + row, 8)

    def across(index, row, by=0):
        return pl.ds(index * block + (1 + by) * rows + row, tiles, stride=rows)

    def wall_at(t, half):
        lanes = pl.ds(pl.multiple_of(t * 128, 128), 128)
        return wall_ref[half * 8 : half * 8 + 8, lanes]

    def pop_at(component, direction, t, half):
        lanes = pl.ds(pl.multiple_of(t * 128, 128), 128)
        return pops[component, direction, half * 8 : half * 8 + 8, lanes].astype(f32)

    rates = [1.0 / value for value in RELAX_TIMES]
    gains = [-3.0 * value / (36.0 * COUPLING) for value in RELAX_TIMES]

    def kept_part(component, fluid, own, bounced):
        kept = 1.0 - rates[component]
        return jnp.where(fluid, kept * own if kept != 0.0 else 0.0, bounced)

    def absorb(t, half, get):
        place = t + 1, HALO + half * 8
        wall = wall_at(t, half)
        fluid = wall == 0
        side = 0 if half == halves - 1 else 1
        densities, momenta = [], []
        for component in range(2):
            total = get(component, 0)
            parts = [None] * 3
            for direction in range(1, 19, 2):
                one, two = get(component, direction), get(component, direction + 1)
                total = total + (one + two)
                gap = one - two
                for axis_pos in range(3):
                    along = velocities[direction][axis_pos]
                    if along != 0:
                        if parts[axis_pos] is None:
                            parts[axis_pos] = gap
                        else:
                            parts[axis_pos] = parts[axis_pos] + gap if along == 1 else parts[axis_pos] - gap
                for toward, own, bounced in ((direction, one, two), (direction + 1, two, one)):
                    if toward in along_x[side]:
                        index = 5 * component + along_x[side].index(toward)
                        start = pl.multiple_of((index * tiles + t) * (size_x + SPARE) + half * 8, 8)
                        held_x[pl.ds(start, 8), :] = kept_part(component, fluid, own, bounced)
            densities.append(total)
            momenta.append(parts)
        strength = jnp.where(
            wall == 1, STRENGTHS[1], jnp.where(wall == 2, STRENGTHS[2], STRENGTHS[3])
        )
        pushes = [COUPLING * (1.0 - jnp.exp(-densities[component])) for component in range(2)]
        field[at(0, *place), :] = jnp.where(fluid, pushes[1], strength)
        field[at(1, *place), :] = jnp.where(fluid, pushes[0], -strength)
        inverse = 3.0 / (densities[0] * rates[0] + densities[1] * rates[1])
        for axis_pos in range(3):
            aux[at(2 + axis_pos, *place), :] = (
                momenta[0][axis_pos] * rates[0] + momenta[1][axis_pos] * rates[1]
            ) * inverse
        for component in range(2):
            gain = gains[component] * pushes[component] / densities[component]
            aux[at(5 + component, *place), :] = jnp.where(fluid, gain, 0.0)
            aux[at(component, *place), :] = jnp.where(fluid, densities[component], 0.0)

    def first_absorb(t, carry):
        load_in(t).wait()
        for half in range(halves):
            absorb(t, half, lambda component, direction: pop_at(component, direction, t, half))
        return carry

    def pack(side, one, two):
        turned = roll(two, NZ)
        return jnp.where(low, turned, one) if side == 0 else jnp.where(low, one, turned)

    def pack_x(step):
        for side in range(2):
            row, inner = (last_row, last_row - 1) if side == 0 else (first_row, first_row + 1)
            for index in range(2):
                send_x[step, side, index] = field[across(index, row), :].astype(bf16)
                send_x[step, side, 2 + index] = field[across(index, inner), :].astype(bf16)
            for index in range(5):
                send_x[step, side, 4 + index] = aux[across(index, row), :].astype(bf16)
            for index in range(10):
                start = index * tiles * (size_x + SPARE) + row - HALO
                part = held_x[pl.ds(start, tiles, stride=size_x + SPARE), :]
                send_x[step, side, 9 + index] = part.astype(bf16)

    def pack_y(step):
        for side in range(2):
            t = tiles - 1 if side == 0 else 0
            for half in range(halves):
                place = t + 1, HALO + half * 8
                fluid = wall_at(t, half) == 0
                for index in range(2):
                    send_y[step, side, half, index] = field[at(index, *place), :].astype(bf16)
                for index, (one, two) in enumerate(((0, 1), (2, 3), (4, 4))):
                    packed = pack(side, aux[at(one, *place), :], aux[at(two, *place), :])
                    send_y[step, side, half, 2 + index] = packed.astype(bf16)
                for index, direction in enumerate(face_order(side, half, halves)):
                    parts = [
                        kept_part(
                            component,
                            fluid,
                            pop_at(component, direction, t, half),
                            pop_at(component, opposite(direction), t, half),
                        )
                        for component in range(2)
                    ]
                    send_y[step, side, half, 5 + index] = pack(side, *parts).astype(bf16)

    def start(step, base, copies):
        started = []
        for place, (source, target, device) in enumerate(copies):
            copy = pltpu.make_async_remote_copy(
                src_ref=source,
                dst_ref=target,
                send_sem=send_sem.at[step, base + place],
                recv_sem=recv_sem.at[step, base + place],
                device_id=device,
                device_id_type=MESH,
            )
            copy.start()
            started.append(copy)
        return started

    def start_y(step):
        copies = []
        for place, (i, j) in enumerate(EDGES):
            source = send_y.at[step, j, halves - 1 if i == 0 else 0, pl.ds(0, EDGE_PARTS)]
            copies.append((source, recv_c.at[step, place], (near_x[i], near_y[j])))
        for side in range(2):
            copies.append((send_y.at[step, side], recv_y.at[step, side], (gx, near_y[side])))
        return start(step, 0, copies)

    def start_x(step):
        copies = []
        for side in range(2):
            copies.append((send_x.at[step, side], recv_x.at[step, side], (near_x[side], gy)))
        return start(step, len(EDGES) + 2, copies)

    def gain_of(component, source, density):
        return jnp.where(density == 0.0, 0.0, gains[component] * source / density)

    def unpack_x(step, side):
        row, outer = (first_row - 1, first_row - 2) if side == 0 else (last_row + 1, last_row + 2)
        sources = []
        for index in range(2):
            source = recv_x[step, side, index].astype(f32)
            sources.append(source)
            field[across(index, row), :] = source
            field[across(index, outer), :] = recv_x[step, side, 2 + index].astype(f32)
        for index in range(5):
            value = recv_x[step, side, 4 + index].astype(f32)
            aux[across(index, row), :] = value
            if index < 2:
                aux[across(5 + index, row), :] = gain_of(index, sources[1 - index], value)

    def unpack_y(side, load, start, order):
        tile = 0 if side == 0 else tiles + 1
        sources = [load(index) for index in range(2)]
        for index in range(2):
            field[at(index, tile, start), :] = sources[index]
        for index, (one, two) in enumerate(((0, 1), (2, 3), (4, None))):
            value = load(2 + index)
            turned = roll(value, NZ)
            aux[at(one, tile, start), :] = value
            if two is not None:
                aux[at(two, tile, start), :] = turned
            if index == 0:
                for component, density in ((0, value), (1, turned)):
                    gain = gain_of(component, sources[1 - component], density)
                    aux[at(5 + component, tile, start), :] = gain
        for index, direction in enumerate(order):
            value = load(5 + index)
            turned = roll(value, NZ)
            place = along_y[side].index(direction)
            for component, part in ((0, value), (1, turned)):
                base = ((5 * component + place) * 2 + side) * rows
                held_y[pl.ds(base + start, 8), :] = part

    def receive_y(step, copies):
        for copy in copies[len(EDGES) : len(EDGES) + 2]:
            copy.wait_recv()
        for side in range(2):
            for half in range(halves):
                unpack_y(
                    side,
                    lambda index: recv_y[step, side, half, index].astype(f32),
                    HALO + half * 8,
                    face_order(side, half, halves),
                )

    def receive_x(step, copies):
        for copy in copies[len(EDGES) + 2 :]:
            copy.wait_recv()
        for side in range(2):
            unpack_x(step, side)

    def receive_corners(step, copies):
        for copy in copies[: len(EDGES)]:
            copy.wait_recv()
        for place, (i, j) in enumerate(EDGES):
            unpack_y(
                j,
                lambda index: recv_c[step, place, index].astype(f32),
                0 if i == 0 else HALO + size_x,
                (along_edge[i, j],),
            )

    inner_windows = tuple(range(first_row, last_row, 8))
    outer_windows = (first_row - 1, last_row - 6)
    middle_windows = tuple(range(first_row + 7, last_row - 6, 8))

    def spread_at(where):
        for index in range(2):
            centre = field[where(index, 0), :]
            above = field[where(index, 1), :]
            below = field[where(index, -1), :]
            gap = above - below
            total = 2.0 * centre + (above + below)
            spread[where(5 * index, 0), :] = gap
            spread[where(5 * index + 1, 0), :] = total
            spread[where(5 * index + 2, 0), :] = roll(gap, NZ)
            spread[where(5 * index + 3, 0), :] = roll(total, NZ)
            spread[where(5 * index + 4, 0), :] = roll(centre, NZ)

    def spread_tile(tile, starts):
        for start in starts:
            spread_at(lambda index, by: off(index, tile, start + by))

    def spread_row(row):
        spread_at(lambda index, by: across(index, row + by))

    def pull_of(index, where):
        def held(kind, by=0):
            return spread[where(5 * index + kind, by), :]

        def upper(here, above):
            return jnp.where(low, here, above)

        def lower(here, below):
            return jnp.where(low, below, here)

        gap = held(0)
        turned_gap = held(2)
        pull_x = 2.0 * gap + (upper(turned_gap, held(2, 1)) + lower(turned_gap, held(2, -1)))
        pull_x = pull_x + (z_from_below(gap, turned_gap) + z_from_above(gap, turned_gap))
        turned_total = held(3)
        pull_y = upper(turned_total, held(3, 1)) - lower(turned_total, held(3, -1))
        turned = held(4)
        y_above = upper(turned, held(4, 1))
        y_below = lower(turned, held(4, -1))
        centre = field[where(index, 0), :]
        turned_y_above = jnp.where(low, field[where(index, 1), :], centre)
        turned_y_below = jnp.where(low, centre, field[where(index, -1), :])
        gap_y = y_above - y_below
        turned_gap_y = turned_y_above - turned_y_below
        pull_y = pull_y + (z_from_below(gap_y, turned_gap_y) + z_from_above(gap_y, turned_gap_y))
        plane = held(1) + (y_above + y_below)
        turned_plane = turned_total + (turned_y_above + turned_y_below)
        pull_z = z_from_above(plane, turned_plane) - z_from_below(plane, turned_plane)
        return pull_x, pull_y, pull_z

    def moved(direction, value):
        _, along, upward = velocities[direction]
        if along != 0 or upward != 0:
            turned = roll(value, NZ)
            if along != 0:
                value, turned = turned, value
            if upward == 1:
                value = z_from_below(value, turned)
            elif upward == -1:
                value = z_from_above(value, turned)
        return value

    def equilibria(component, where, directions, left_out=None):
        pull = pull_of(component, where)
        density = aux[where(component, 0), :]
        if left_out is not None:
            density = jnp.where(left_out, 0.0, density)
        gain = aux[where(5 + component, 0), :]
        speed = [aux[where(2 + axis_pos, 0), :] + gain * pull[axis_pos] for axis_pos in range(3)]
        square = speed[0] * speed[0] + speed[1] * speed[1] + speed[2] * speed[2]
        level = 1.0 - square * (1.0 / 6.0)
        light = density * (rates[component] / 36.0)
        heavy = density * (rates[component] / 18.0)
        light_level = light * level
        heavy_level = heavy * level
        if 0 in directions:
            yield 0, 6.0 * heavy_level
        for direction in range(1, 19, 2):
            if direction not in directions and direction + 1 not in directions:
                continue
            along = None
            for axis_pos in range(3):
                part = velocities[direction][axis_pos]
                if part == 1:
                    along = speed[axis_pos] if along is None else along + speed[axis_pos]
                elif part == -1:
                    along = along - speed[axis_pos]
            weighted = (heavy if direction < 7 else light) * along
            even = (heavy_level if direction < 7 else light_level) + 0.5 * (weighted * along)
            if direction in directions:
                yield direction, even + weighted
            if direction + 1 in directions:
                yield direction + 1, even - weighted

    def collide(t):
        for half in range(halves):
            fluid = wall_at(t, half) == 0
            left_out = row_index == (7 if half == halves - 1 else 0)

            def where(index, by):
                return at(index, t + 1 + by, HALO + half * 8)

            for component in range(2):
                kept = 1.0 - rates[component]
                for direction, relaxed in equilibria(component, where, range(19), left_out):
                    if kept != 0.0:
                        relaxed = relaxed + kept * pop_at(component, direction, t, half)
                    bounced = pop_at(component, opposite(direction), t, half)
                    value = moved(direction, jnp.where(fluid, relaxed, bounced))
                    stream[where(19 * component + direction, 0), :] = value

    def collide_row(row):
        for component in range(2):

            def where(index, by):
                return across(index, row, by)

            for direction, relaxed in equilibria(component, where, range(19)):
                place = where(19 * component + direction, 0)
                stream[place, :] = stream[place, :] + moved(direction, relaxed)

    def collide_outside_x(step, side):
        row = first_row - 1 if side == 0 else last_row + 1
        for component in range(2):

            def where(index, by):
                return across(index, row, by)

            for direction, relaxed in equilibria(component, where, along_x[side]):
                place = 5 * component + along_x[side].index(direction)
                value = relaxed + recv_x[step, side, 9 + place].astype(f32)
                stream[where(19 * component + direction, 0), :] = moved(direction, value)

    def collide_outside_y(side, starts):
        tile = 0 if side == 0 else tiles + 1
        for start in starts:
            for component in range(2):

                def where(index, by):
                    return off(index, min(max(tile + by, 0), tiles + 1), start)

                for direction, relaxed in equilibria(component, where, along_y[side]):
                    place = 5 * component + along_y[side].index(direction)
                    part = held_y[pl.ds((place * 2 + side) * rows + start, 8), :]
                    value = moved(direction, relaxed + part)
                    stream[where(19 * component + direction, 0), :] = value

    def settle_step(last, first_tile, last_tile, stride):
        target = out_ref if last else pops

        def read(t):
            lanes = pl.ds(pl.multiple_of(t * 128, 128), 128)
            for half in range(halves):
                fluid = wall_at(t, half) == 0
                xglobal = gx * size_x + half * 8 + row_index
                inlet = jnp.logical_and(xglobal == planes_ref[0], fluid)
                outlet = jnp.logical_and(xglobal == planes_ref[1], fluid)
                fixed = jnp.logical_or(inlet, outlet)
                forced = [{}, {}]
                for component in range(2):
                    for weight in sorted(set(lattice_weights)):
                        values = [
                            float(np.asarray(weight * level[component], bf16))
                            for level in (INLET_DENSITY, OUTLET_DENSITY)
                        ]
                        forced[component][weight] = jnp.where(inlet, values[0], values[1])

                def get(component, direction):
                    step_x, step_y, _ = velocities[direction]
                    index = 19 * component + direction
                    start = HALO + half * 8 - step_x
                    value = stream[off(index, t + 1, start), :]
                    if step_y == 1:
                        value = jnp.where(low, stream[off(index, t, start), :], value)
                    elif step_y == -1:
                        value = jnp.where(low, value, stream[off(index, t + 2, start), :])
                    value = jnp.where(fixed, forced[component][lattice_weights[direction]], value)
                    narrow = value.astype(bf16)
                    target[component, direction, half * 8 : half * 8 + 8, lanes] = narrow
                    return narrow.astype(f32)

                if last:
                    for component in range(2):
                        for direction in range(19):
                            get(component, direction)
                else:
                    absorb(t, half, get)

        each_tile(first_tile, last_tile, stride, read)

    def clear(tile, carry):
        for index in range(2):
            for start in (0, HALO + size_x):
                field[at(index, tile, start), :] = jnp.zeros((8, 128), f32)
        return carry

    def each_tile(first, last, step, work):
        def body(k, carry):
            work(first + k * step)
            return carry

        lax.fori_loop(0, (last - first) // step + 1, body, 0)

    lax.fori_loop(0, tiles + 2, clear, 0)
    load_wall.wait()
    lax.fori_loop(0, tiles, first_absorb, 0)
    load_planes.wait()
    pack_y(0)
    pack_x(0)
    pl.semaphore_wait(barrier, len(targets))
    copies = start_y(0) + start_x(0)
    sent = []
    for step in range(STEPS):
        sent += copies
        each_tile(1, tiles, 1, lambda tile: spread_tile(tile, inner_windows))
        each_tile(1, tiles - 2, 1, collide)
        receive_y(step, copies)
        each_tile(0, tiles + 1, tiles + 1, lambda tile: spread_tile(tile, inner_windows))
        each_tile(0, tiles - 1, tiles - 1, collide)
        for side in range(2):
            collide_outside_y(side, middle_windows)
        receive_x(step, copies)
        for row in (first_row - 1, first_row, last_row, last_row + 1):
            spread_row(row)
        receive_corners(step, copies)
        each_tile(0, tiles + 1, tiles + 1, lambda tile: spread_tile(tile, outer_windows))
        for side in range(2):
            collide_outside_y(side, outer_windows)
            collide_outside_x(step, side)
        each_tile(first_row, last_row, last_row - first_row, collide_row)
        if step == STEPS - 1:
            settle_step(True, 0, tiles - 1, 1)
        else:
            settle_step(False, 0, tiles - 1, tiles - 1)
            pack_y(step + 1)
            copies = start_y(step + 1)
            settle_step(False, 1, tiles - 2, 1)
            pack_x(step + 1)
            copies = copies + start_x(step + 1)
    for copy in sent:
        copy.wait_send()


def on_device(nx_devices, ny_devices, populations, wall_class, planes):
    size_x, width = populations.shape[2:]
    tiles = width // 128
    halves = size_x // 8
    rows = size_x + 2 * HALO + SPARE
    block = (tiles + 2) * rows
    bf16 = jnp.bfloat16
    f32 = jnp.float32
    return pl.pallas_call(
        functools.partial(kernel, nx_devices, ny_devices),
        out_shape=jax.ShapeDtypeStruct(populations.shape, bf16),
        in_specs=[pl.BlockSpec(memory_space=pltpu.HBM)] * 3,
        out_specs=pl.BlockSpec(memory_space=pltpu.VMEM),
        scratch_shapes=[
            pltpu.VMEM(populations.shape, bf16),
            pltpu.VMEM(wall_class.shape, wall_class.dtype),
            pltpu.SMEM(planes.shape, planes.dtype),
            pltpu.VMEM((2 * block, 128), f32),
            pltpu.VMEM((10 * block, 128), f32),
            pltpu.VMEM((7 * block, 128), f32),
            pltpu.VMEM((10 * tiles * (size_x + SPARE), 128), f32),
            pltpu.VMEM((20 * rows, 128), f32),
            pltpu.VMEM((38 * block, 128), f32),
            pltpu.VMEM((STEPS, 2, X_PARTS, tiles, 128), bf16),
            pltpu.VMEM((STEPS, 2, halves, Y_PARTS, 8, 128), bf16),
            pltpu.VMEM((STEPS, 2, X_PARTS, tiles, 128), bf16),
            pltpu.VMEM((STEPS, 2, halves, Y_PARTS, 8, 128), bf16),
            pltpu.VMEM((STEPS, 4, EDGE_PARTS, 8, 128), bf16),
            pltpu.SemaphoreType.DMA((tiles + 2,)),
            pltpu.SemaphoreType.DMA((STEPS, 8)),
            pltpu.SemaphoreType.DMA((STEPS, 8)),
        ],
        compiler_params=pltpu.CompilerParams(
            collective_id=0, has_side_effects=True, vmem_limit_bytes=40 * 1024 * 1024
        ),
    )(*[pltpu.with_memory_space_constraint(v, pltpu.HBM) for v in (populations, wall_class, planes)])


def solution(mesh):
    in_specs = (P(None, None, "gx", "gy"), P("gx", "gy"), P())
    out_specs = P(None, None, "gx", "gy")
    return jax.shard_map(
        functools.partial(on_device, mesh.shape["gx"], mesh.shape["gy"]),
        mesh=mesh,
        in_specs=in_specs,
        out_specs=out_specs,
        check_vma=False,
    )
```

```python
import functools

import jax
import jax.numpy as jnp
import numpy as np
from jax import lax
from jax.experimental import pallas as pl
from jax.experimental.pallas import tpu as pltpu
from jax.sharding import PartitionSpec as P

NZ = 64
STEPS = 2
MESH = pl.DeviceIdType.MESH
velocities = (
    (0, 0, 0),
    (1, 0, 0),
    (-1, 0, 0),
    (0, 1, 0),
    (0, -1, 0),
    (0, 0, 1),
    (0, 0, -1),
    (1, 1, 0),
    (-1, -1, 0),
    (1, -1, 0),
    (-1, 1, 0),
    (1, 0, 1),
    (-1, 0, -1),
    (1, 0, -1),
    (-1, 0, 1),
    (0, 1, 1),
    (0, -1, -1),
    (0, 1, -1),
    (0, -1, 1),
)
lattice_weights = (1.0 / 3.0,) + (1.0 / 18.0,) * 6 + (1.0 / 36.0,) * 12
COUPLING = 2.5
RELAX_TIMES = (1.0, 0.8)
STRENGTHS = (0.0, 0.15, 0.35, 0.6)
INLET_DENSITY = (1.0, 0.03)
OUTLET_DENSITY = (0.03, 1.0)
along_x = ((1, 7, 9, 11, 13), (2, 8, 10, 12, 14))
along_y = ((3, 7, 10, 15, 17), (4, 8, 9, 16, 18))
along_edge = {(0, 0): 7, (1, 1): 8, (0, 1): 9, (1, 0): 10}
EDGES = ((0, 0), (0, 1), (1, 0), (1, 1))

HALO = 8
SPARE = 8


def opposite(direction):
    if direction == 0:
        return 0
    return direction + 1 if direction % 2 == 1 else direction - 1


def face_order(side, half, halves):
    edge = along_edge[0 if half == halves - 1 else 1, side]
    return (edge,) + tuple(d for d in along_y[side] if d != edge)


X_PARTS = 4 + 5 + 10
Y_PARTS = 2 + 3 + 5
EDGE_PARTS = 2 + 3 + 1


def kernel(
    nx_devices,
    ny_devices,
    pops_hbm,
    wall_hbm,
    planes_hbm,
    out_ref,
    pops,
    wall_ref,
    planes_ref,
    field,
    spread,
    aux,
    held_x,
    held_y,
    stream,
    send_x,
    send_y,
    recv_x,
    recv_y,
    recv_c,
    in_sem,
    send_sem,
    recv_sem,
):
    size_x = pops.shape[2]
    tiles = pops.shape[3] // 128
    halves = size_x // 8
    rows = size_x + 2 * HALO + SPARE
    block = (tiles + 2) * rows
    first_row = HALO
    last_row = HALO + size_x - 1
    f32 = jnp.float32
    bf16 = jnp.bfloat16

    gx = lax.axis_index("gx")
    gy = lax.axis_index("gy")
    near_x = (lax.rem(gx + 1, nx_devices), lax.rem(gx + nx_devices - 1, nx_devices))
    near_y = (lax.rem(gy + 1, ny_devices), lax.rem(gy + ny_devices - 1, ny_devices))

    barrier = pltpu.get_barrier_semaphore()
    targets = [(near_x[i], near_y[j]) for i, j in EDGES]
    targets += [(near_x[0], gy), (near_x[1], gy), (gx, near_y[0]), (gx, near_y[1])]
    for target in targets:
        pl.semaphore_signal(barrier, inc=1, device_id=target, device_id_type=MESH)

    def load_in(t):
        lanes = pl.ds(pl.multiple_of(t * 128, 128), 128)
        return pltpu.make_async_copy(
            pops_hbm.at[:, :, :, lanes], pops.at[:, :, :, lanes], in_sem.at[t]
        )

    load_wall = pltpu.make_async_copy(wall_hbm, wall_ref, in_sem.at[tiles])
    load_planes = pltpu.make_async_copy(planes_hbm, planes_ref, in_sem.at[tiles + 1])
    load_wall.start()
    for t in range(tiles):
        load_in(t).start()
    load_planes.start()

    lane = lax.broadcasted_iota(jnp.int32, (8, 128), 1)
    row_index = lax.broadcasted_iota(jnp.int32, (8, 128), 0)
    low = lane < NZ
    first_z = jnp.logical_or(lane == 0, lane == NZ)
    last_z = jnp.logical_or(lane == NZ - 1, lane == 2 * NZ - 1)

    def roll(value, by):
        return pltpu.roll(value, by % 128, 1)

    def z_from_below(value, turned):
        return roll(jnp.where(last_z, turned, value), 1)

    def z_from_above(value, turned):
        return roll(jnp.where(first_z, turned, value), -1)

    def at(index, tile, row):
        return pl.ds(pl.multiple_of(index * block + tile * rows + row, 8), 8)

    def off(index, tile, row):
        return pl.ds(index * block + tile * rows + row, 8)

    def across(index, row, by=0):
        return pl.ds(index * block + (1 + by) * rows + row, tiles, stride=rows)

    def wall_at(t, half):
        lanes = pl.ds(pl.multiple_of(t * 128, 128), 128)
        return wall_ref[half * 8 : half * 8 + 8, lanes]

    def pop_at(component, direction, t, half):
        lanes = pl.ds(pl.multiple_of(t * 128, 128), 128)
        return pops[component, direction, half * 8 : half * 8 + 8, lanes].astype(f32)

    rates = [1.0 / value for value in RELAX_TIMES]
    gains = [-3.0 * value / (36.0 * COUPLING) for value in RELAX_TIMES]

    def kept_part(component, fluid, own, bounced):
        kept = 1.0 - rates[component]
        return jnp.where(fluid, kept * own if kept != 0.0 else 0.0, bounced)

    def absorb(t, half, get):
        place = t + 1, HALO + half * 8
        wall = wall_at(t, half)
        fluid = wall == 0
        side = 0 if half == halves - 1 else 1
        densities, momenta = [], []
        for component in range(2):
            total = get(component, 0)
            parts = [None] * 3
            for direction in range(1, 19, 2):
                one, two = get(component, direction), get(component, direction + 1)
                total = total + (one + two)
                gap = one - two
                for axis_pos in range(3):
                    along = velocities[direction][axis_pos]
                    if along != 0:
                        if parts[axis_pos] is None:
                            parts[axis_pos] = gap
                        else:
                            parts[axis_pos] = parts[axis_pos] + gap if along == 1 else parts[axis_pos] - gap
                for toward, own, bounced in ((direction, one, two), (direction + 1, two, one)):
                    if toward in along_x[side]:
                        index = 5 * component + along_x[side].index(toward)
                        start = pl.multiple_of((index * tiles + t) * (size_x + SPARE) + half * 8, 8)
                        held_x[pl.ds(start, 8), :] = kept_part(component, fluid, own, bounced)
            densities.append(total)
            momenta.append(parts)
        strength = jnp.where(
            wall == 1, STRENGTHS[1], jnp.where(wall == 2, STRENGTHS[2], STRENGTHS[3])
        )
        pushes = [COUPLING * (1.0 - jnp.exp(-densities[component])) for component in range(2)]
        field[at(0, *place), :] = jnp.where(fluid, pushes[1], strength)
        field[at(1, *place), :] = jnp.where(fluid, pushes[0], -strength)
        inverse = 3.0 / (densities[0] * rates[0] + densities[1] * rates[1])
        for axis_pos in range(3):
            aux[at(2 + axis_pos, *place), :] = (
                momenta[0][axis_pos] * rates[0] + momenta[1][axis_pos] * rates[1]
            ) * inverse
        for component in range(2):
            gain = gains[component] * pushes[component] / densities[component]
            aux[at(5 + component, *place), :] = jnp.where(fluid, gain, 0.0)
            aux[at(component, *place), :] = jnp.where(fluid, densities[component], 0.0)

    def first_absorb(t, carry):
        load_in(t).wait()
        for half in range(halves):
            absorb(t, half, lambda component, direction: pop_at(component, direction, t, half))
        return carry

    def pack(side, one, two):
        turned = roll(two, NZ)
        return jnp.where(low, turned, one) if side == 0 else jnp.where(low, one, turned)

    def pack_x(step):
        for side in range(2):
            row, inner = (last_row, last_row - 1) if side == 0 else (first_row, first_row + 1)
            for index in range(2):
                send_x[step, side, index] = field[across(index, row), :].astype(bf16)
                send_x[step, side, 2 + index] = field[across(index, inner), :].astype(bf16)
            for index in range(5):
                send_x[step, side, 4 + index] = aux[across(index, row), :].astype(bf16)
            for index in range(10):
                start = index * tiles * (size_x + SPARE) + row - HALO
                part = held_x[pl.ds(start, tiles, stride=size_x + SPARE), :]
                send_x[step, side, 9 + index] = part.astype(bf16)

    def pack_y(step):
        for side in range(2):
            t = tiles - 1 if side == 0 else 0
            for half in range(halves):
                place = t + 1, HALO + half * 8
                fluid = wall_at(t, half) == 0
                for index in range(2):
                    send_y[step, side, half, index] = field[at(index, *place), :].astype(bf16)
                for index, (one, two) in enumerate(((0, 1), (2, 3), (4, 4))):
                    packed = pack(side, aux[at(one, *place), :], aux[at(two, *place), :])
                    send_y[step, side, half, 2 + index] = packed.astype(bf16)
                for index, direction in enumerate(face_order(side, half, halves)):
                    parts = [
                        kept_part(
                            component,
                            fluid,
                            pop_at(component, direction, t, half),
                            pop_at(component, opposite(direction), t, half),
                        )
                        for component in range(2)
                    ]
                    send_y[step, side, half, 5 + index] = pack(side, *parts).astype(bf16)

    def start(step, base, copies):
        started = []
        for place, (source, target, device) in enumerate(copies):
            copy = pltpu.make_async_remote_copy(
                src_ref=source,
                dst_ref=target,
                send_sem=send_sem.at[step, base + place],
                recv_sem=recv_sem.at[step, base + place],
                device_id=device,
                device_id_type=MESH,
            )
            copy.start()
            started.append(copy)
        return started

    def start_y(step):
        copies = []
        for place, (i, j) in enumerate(EDGES):
            source = send_y.at[step, j, halves - 1 if i == 0 else 0, pl.ds(0, EDGE_PARTS)]
            copies.append((source, recv_c.at[step, place], (near_x[i], near_y[j])))
        for side in range(2):
            copies.append((send_y.at[step, side], recv_y.at[step, side], (gx, near_y[side])))
        return start(step, 0, copies)

    def start_x(step):
        copies = []
        for side in range(2):
            copies.append((send_x.at[step, side], recv_x.at[step, side], (near_x[side], gy)))
        return start(step, len(EDGES) + 2, copies)

    def gain_of(component, source, density):
        return jnp.where(density == 0.0, 0.0, gains[component] * source / density)

    def unpack_x(step, side):
        row, outer = (first_row - 1, first_row - 2) if side == 0 else (last_row + 1, last_row + 2)
        sources = []
        for index in range(2):
            source = recv_x[step, side, index].astype(f32)
            sources.append(source)
            field[across(index, row), :] = source
            field[across(index, outer), :] = recv_x[step, side, 2 + index].astype(f32)
        for index in range(5):
            value = recv_x[step, side, 4 + index].astype(f32)
            aux[across(index, row), :] = value
            if index < 2:
                aux[across(5 + index, row), :] = gain_of(index, sources[1 - index], value)

    def unpack_y(side, load, start, order):
        tile = 0 if side == 0 else tiles + 1
        sources = [load(index) for index in range(2)]
        for index in range(2):
            field[at(index, tile, start), :] = sources[index]
        for index, (one, two) in enumerate(((0, 1), (2, 3), (4, None))):
            value = load(2 + index)
            turned = roll(value, NZ)
            aux[at(one, tile, start), :] = value
            if two is not None:
                aux[at(two, tile, start), :] = turned
            if index == 0:
                for component, density in ((0, value), (1, turned)):
                    gain = gain_of(component, sources[1 - component], density)
                    aux[at(5 + component, tile, start), :] = gain
        for index, direction in enumerate(order):
            value = load(5 + index)
            turned = roll(value, NZ)
            place = along_y[side].index(direction)
            for component, part in ((0, value), (1, turned)):
                base = ((5 * component + place) * 2 + side) * rows
                held_y[pl.ds(base + start, 8), :] = part

    def receive_y(step, copies):
        for copy in copies[len(EDGES) : len(EDGES) + 2]:
            copy.wait_recv()
        for side in range(2):
            for half in range(halves):
                unpack_y(
                    side,
                    lambda index: recv_y[step, side, half, index].astype(f32),
                    HALO + half * 8,
                    face_order(side, half, halves),
                )

    def receive_x(step, copies):
        for copy in copies[len(EDGES) + 2 :]:
            copy.wait_recv()
        for side in range(2):
            unpack_x(step, side)

    def receive_corners(step, copies):
        for copy in copies[: len(EDGES)]:
            copy.wait_recv()
        for place, (i, j) in enumerate(EDGES):
            unpack_y(
                j,
                lambda index: recv_c[step, place, index].astype(f32),
                0 if i == 0 else HALO + size_x,
                (along_edge[i, j],),
            )

    inner_windows = tuple(range(first_row, last_row, 8))
    outer_windows = (first_row - 1, last_row - 6)
    middle_windows = tuple(range(first_row + 7, last_row - 6, 8))

    def spread_at(where):
        for index in range(2):
            centre = field[where(index, 0), :]
            above = field[where(index, 1), :]
            below = field[where(index, -1), :]
            gap = above - below
            total = 2.0 * centre + (above + below)
            spread[where(5 * index, 0), :] = gap
            spread[where(5 * index + 1, 0), :] = total
            spread[where(5 * index + 2, 0), :] = roll(gap, NZ)
            spread[where(5 * index + 3, 0), :] = roll(total, NZ)
            spread[where(5 * index + 4, 0), :] = roll(centre, NZ)

    def spread_tile(tile, starts):
        for start in starts:
            spread_at(lambda index, by: (off if (start + by) % 8 else at)(index, tile, start + by))

    def spread_row(row):
        spread_at(lambda index, by: across(index, row + by))

    def pull_of(index, where):
        def held(kind, by=0):
            return spread[where(5 * index + kind, by), :]

        def upper(here, above):
            return jnp.where(low, here, above)

        def lower(here, below):
            return jnp.where(low, below, here)

        gap = held(0)
        turned_gap = held(2)
        pull_x = 2.0 * gap + (upper(turned_gap, held(2, 1)) + lower(turned_gap, held(2, -1)))
        pull_x = pull_x + (z_from_below(gap, turned_gap) + z_from_above(gap, turned_gap))
        turned_total = held(3)
        pull_y = upper(turned_total, held(3, 1)) - lower(turned_total, held(3, -1))
        turned = held(4)
        y_above = upper(turned, held(4, 1))
        y_below = lower(turned, held(4, -1))
        centre = field[where(index, 0), :]
        turned_y_above = jnp.where(low, field[where(index, 1), :], centre)
        turned_y_below = jnp.where(low, centre, field[where(index, -1), :])
        gap_y = y_above - y_below
        turned_gap_y = turned_y_above - turned_y_below
        pull_y = pull_y + (z_from_below(gap_y, turned_gap_y) + z_from_above(gap_y, turned_gap_y))
        plane = held(1) + (y_above + y_below)
        turned_plane = turned_total + (turned_y_above + turned_y_below)
        pull_z = z_from_above(plane, turned_plane) - z_from_below(plane, turned_plane)
        return pull_x, pull_y, pull_z

    def moved(direction, value):
        _, along, upward = velocities[direction]
        if along != 0 or upward != 0:
            turned = roll(value, NZ)
            if along != 0:
                value, turned = turned, value
            if upward == 1:
                value = z_from_below(value, turned)
            elif upward == -1:
                value = z_from_above(value, turned)
        return value

    def equilibria(component, where, directions, left_out=None):
        pull = pull_of(component, where)
        density = aux[where(component, 0), :]
        if left_out is not None:
            density = jnp.where(left_out, 0.0, density)
        gain = aux[where(5 + component, 0), :]
        speed = [aux[where(2 + axis_pos, 0), :] + gain * pull[axis_pos] for axis_pos in range(3)]
        square = speed[0] * speed[0] + speed[1] * speed[1] + speed[2] * speed[2]
        level = 1.0 - square * (1.0 / 6.0)
        light = density * (rates[component] / 36.0)
        heavy = density * (rates[component] / 18.0)
        light_level = light * level
        heavy_level = heavy * level
        if 0 in directions:
            yield 0, 6.0 * heavy_level
        for direction in range(1, 19, 2):
            if direction not in directions and direction + 1 not in directions:
                continue
            along = None
            for axis_pos in range(3):
                part = velocities[direction][axis_pos]
                if part == 1:
                    along = speed[axis_pos] if along is None else along + speed[axis_pos]
                elif part == -1:
                    along = along - speed[axis_pos]
            weighted = (heavy if direction < 7 else light) * along
            even = (heavy_level if direction < 7 else light_level) + 0.5 * (weighted * along)
            if direction in directions:
                yield direction, even + weighted
            if direction + 1 in directions:
                yield direction + 1, even - weighted

    def collide(t):
        for half in range(halves):
            fluid = wall_at(t, half) == 0
            left_out = row_index == (7 if half == halves - 1 else 0)

            def where(index, by):
                return at(index, t + 1 + by, HALO + half * 8)

            for component in range(2):
                kept = 1.0 - rates[component]
                for direction, relaxed in equilibria(component, where, range(19), left_out):
                    if kept != 0.0:
                        relaxed = relaxed + kept * pop_at(component, direction, t, half)
                    bounced = pop_at(component, opposite(direction), t, half)
                    value = moved(direction, jnp.where(fluid, relaxed, bounced))
                    stream[where(19 * component + direction, 0), :] = value

    def collide_row(row):
        for component in range(2):

            def where(index, by):
                return across(index, row, by)

            for direction, relaxed in equilibria(component, where, range(19)):
                place = where(19 * component + direction, 0)
                stream[place, :] = stream[place, :] + moved(direction, relaxed)

    def collide_outside_x(step, side):
        row = first_row - 1 if side == 0 else last_row + 1
        for component in range(2):

            def where(index, by):
                return across(index, row, by)

            for direction, relaxed in equilibria(component, where, along_x[side]):
                place = 5 * component + along_x[side].index(direction)
                value = relaxed + recv_x[step, side, 9 + place].astype(f32)
                stream[where(19 * component + direction, 0), :] = moved(direction, value)

    def collide_outside_y(side, starts):
        tile = 0 if side == 0 else tiles + 1
        for start in starts:
            for component in range(2):

                def where(index, by):
                    return off(index, min(max(tile + by, 0), tiles + 1), start)

                for direction, relaxed in equilibria(component, where, along_y[side]):
                    place = 5 * component + along_y[side].index(direction)
                    part = held_y[pl.ds((place * 2 + side) * rows + start, 8), :]
                    value = moved(direction, relaxed + part)
                    stream[where(19 * component + direction, 0), :] = value

    def settle_step(last, first_tile, last_tile, stride):
        target = out_ref if last else pops

        def read(t):
            lanes = pl.ds(pl.multiple_of(t * 128, 128), 128)
            for half in range(halves):
                fluid = wall_at(t, half) == 0
                xglobal = gx * size_x + half * 8 + row_index
                inlet = jnp.logical_and(xglobal == planes_ref[0], fluid)
                outlet = jnp.logical_and(xglobal == planes_ref[1], fluid)
                fixed = jnp.logical_or(inlet, outlet)
                forced = [{}, {}]
                for component in range(2):
                    for weight in sorted(set(lattice_weights)):
                        values = [
                            float(np.asarray(weight * level[component], bf16))
                            for level in (INLET_DENSITY, OUTLET_DENSITY)
                        ]
                        forced[component][weight] = jnp.where(inlet, values[0], values[1])

                def get(component, direction):
                    step_x, step_y, _ = velocities[direction]
                    index = 19 * component + direction
                    start = HALO + half * 8 - step_x
                    rows_of = off if step_x else at
                    value = stream[rows_of(index, t + 1, start), :]
                    if step_y == 1:
                        value = jnp.where(low, stream[rows_of(index, t, start), :], value)
                    elif step_y == -1:
                        value = jnp.where(low, value, stream[rows_of(index, t + 2, start), :])
                    value = jnp.where(fixed, forced[component][lattice_weights[direction]], value)
                    narrow = value.astype(bf16)
                    target[component, direction, half * 8 : half * 8 + 8, lanes] = narrow
                    return narrow.astype(f32)

                if last:
                    for component in range(2):
                        for direction in range(19):
                            get(component, direction)
                else:
                    absorb(t, half, get)

        each_tile(first_tile, last_tile, stride, read)

    def clear(tile, carry):
        for index in range(2):
            for start in (0, HALO + size_x):
                field[at(index, tile, start), :] = jnp.zeros((8, 128), f32)
        return carry

    def each_tile(first, last, step, work):
        def body(k, carry):
            work(first + k * step)
            return carry

        lax.fori_loop(0, (last - first) // step + 1, body, 0)

    lax.fori_loop(0, tiles + 2, clear, 0)
    load_wall.wait()
    lax.fori_loop(0, tiles, first_absorb, 0)
    load_planes.wait()
    pack_y(0)
    pack_x(0)
    pl.semaphore_wait(barrier, len(targets))
    copies = start_y(0) + start_x(0)
    sent = []
    for step in range(STEPS):
        sent += copies
        each_tile(1, tiles, 1, lambda tile: spread_tile(tile, inner_windows))
        each_tile(1, tiles - 2, 1, collide)
        receive_y(step, copies)
        each_tile(0, tiles + 1, tiles + 1, lambda tile: spread_tile(tile, inner_windows))
        each_tile(0, tiles - 1, tiles - 1, collide)
        for side in range(2):
            collide_outside_y(side, middle_windows)
        receive_x(step, copies)
        for row in (first_row - 1, first_row, last_row, last_row + 1):
            spread_row(row)
        receive_corners(step, copies)
        each_tile(0, tiles + 1, tiles + 1, lambda tile: spread_tile(tile, outer_windows))
        for side in range(2):
            collide_outside_y(side, outer_windows)
            collide_outside_x(step, side)
        each_tile(first_row, last_row, last_row - first_row, collide_row)
        if step == STEPS - 1:
            settle_step(True, 0, tiles - 1, 1)
        else:
            settle_step(False, 0, tiles - 1, tiles - 1)
            pack_y(step + 1)
            copies = start_y(step + 1)
            settle_step(False, 1, tiles - 2, 1)
            pack_x(step + 1)
            copies = copies + start_x(step + 1)
    for copy in sent:
        copy.wait_send()


def on_device(nx_devices, ny_devices, populations, wall_class, planes):
    size_x, width = populations.shape[2:]
    tiles = width // 128
    halves = size_x // 8
    rows = size_x + 2 * HALO + SPARE
    block = (tiles + 2) * rows
    bf16 = jnp.bfloat16
    f32 = jnp.float32
    return pl.pallas_call(
        functools.partial(kernel, nx_devices, ny_devices),
        out_shape=jax.ShapeDtypeStruct(populations.shape, bf16),
        in_specs=[pl.BlockSpec(memory_space=pltpu.HBM)] * 3,
        out_specs=pl.BlockSpec(memory_space=pltpu.VMEM),
        scratch_shapes=[
            pltpu.VMEM(populations.shape, bf16),
            pltpu.VMEM(wall_class.shape, wall_class.dtype),
            pltpu.SMEM(planes.shape, planes.dtype),
            pltpu.VMEM((2 * block, 128), f32),
            pltpu.VMEM((10 * block, 128), f32),
            pltpu.VMEM((7 * block, 128), f32),
            pltpu.VMEM((10 * tiles * (size_x + SPARE), 128), f32),
            pltpu.VMEM((20 * rows, 128), f32),
            pltpu.VMEM((38 * block, 128), f32),
            pltpu.VMEM((STEPS, 2, X_PARTS, tiles, 128), bf16),
            pltpu.VMEM((STEPS, 2, halves, Y_PARTS, 8, 128), bf16),
            pltpu.VMEM((STEPS, 2, X_PARTS, tiles, 128), bf16),
            pltpu.VMEM((STEPS, 2, halves, Y_PARTS, 8, 128), bf16),
            pltpu.VMEM((STEPS, 4, EDGE_PARTS, 8, 128), bf16),
            pltpu.SemaphoreType.DMA((tiles + 2,)),
            pltpu.SemaphoreType.DMA((STEPS, 8)),
            pltpu.SemaphoreType.DMA((STEPS, 8)),
        ],
        compiler_params=pltpu.CompilerParams(
            collective_id=0, has_side_effects=True, vmem_limit_bytes=40 * 1024 * 1024
        ),
    )(*[pltpu.with_memory_space_constraint(v, pltpu.HBM) for v in (populations, wall_class, planes)])


def solution(mesh):
    in_specs = (P(None, None, "gx", "gy"), P("gx", "gy"), P())
    out_specs = P(None, None, "gx", "gy")
    return jax.shard_map(
        functools.partial(on_device, mesh.shape["gx"], mesh.shape["gy"]),
        mesh=mesh,
        in_specs=in_specs,
        out_specs=out_specs,
        check_vma=False,
    )
```
